128 devices in a mesh: rows: 8 (over z, core), cols: 16 (over x, y).
Axes of the slice: x: 4, y: 4, z: 4, core: 2. Of those that a mesh axis runs over, the one named last changes fastest.
Arguments:
- embeddings: bfloat16 [917504, 1024], P(('rows', 'cols'))
- factor_cols: bfloat16 [917504, 512], P(('rows', 'cols')), may hold values from -0.12 to 0.12, as said below
- solved: int32 [917504], P(('rows', 'cols')), may hold values from 0 to 16
- pivots: int32 [256], replicated, may hold values from 0 to 917503, as said below
Outputs:
- new_cols: bfloat16 [917504, 256], P(('rows', 'cols'))
- gains: float32 [917504], P(('rows', 'cols'))
- best_gain: float32 [], replicated
The draws below stay inside these ranges and needn't reach their ends.
Inputs may be any that keep to these rules, and one draw needn't show every extreme that they name: `pivots`: 256 distinct row numbers in increasing order; the 7168 consecutive rows of one device hold at most 16 of them, and some device holds exactly 16. `factor_cols`: the pivots' factor rows F satisfy: every eigenvalue of F F^T is below 1.
All inputs are finite; a program needn't handle non-finite values.
Results may differ from the reference program's by a relative error of at most 0.001.
Values may be sent and summed in bfloat16 or wider, within the bound.
No kernel may reach another device: no remote copies, remote signals or barrier semaphores. Data moves between devices by JAX's collectives and lax.ppermute only.
A program may use at most 128 MiB of HBM per device.

```python
import jax
import jax.numpy as jnp
from jax import lax

D = 1024
K0 = 512
P_SIZE = 256
PMAX = 16
ROWS_DEV = 7168
NUM_ROWS = 917504


def draw_embeddings(key, part):
    base = jax.random.fold_in(key, 11)
    k_noise, k_shared, k_amp = jax.random.split(base, 3)
    shared = jax.random.normal(k_shared, (D,), jnp.float32)
    noise = jax.random.normal(k_noise, (NUM_ROWS, D), jnp.float32)
    amp = jax.random.uniform(k_amp, (NUM_ROWS, 1), jnp.float32, 0.5, 2.0)
    return (noise + amp * shared[None, :]).astype(jnp.bfloat16)


def draw_factor_cols(key, part):
    base = jax.random.fold_in(key, 37)
    k_noise = jax.random.fold_in(base, 0)
    values = jnp.clip(0.02 * jax.random.normal(k_noise, (NUM_ROWS, K0), jnp.float32), -0.12, 0.12)
    return values.astype(jnp.bfloat16)


def draw_pivots(key, part):
    base = jax.random.fold_in(key, 23)
    devices = NUM_ROWS // ROWS_DEV
    k_heavy, k_perm, k_offset = jax.random.split(base, 3)
    heavy = jax.random.randint(k_heavy, (), 0, devices).astype(jnp.int32)
    others = jax.random.permutation(k_perm, (devices - 1) * PMAX)[:P_SIZE - PMAX].astype(jnp.int32)
    owner = others // PMAX
    owner = owner + (owner >= heavy).astype(jnp.int32)
    slot_other = owner * PMAX + others % PMAX
    slot_heavy = heavy * PMAX + jnp.arange(PMAX, dtype=jnp.int32)
    slots = jnp.sort(jnp.concatenate([slot_heavy, slot_other]))
    spacing = ROWS_DEV // PMAX
    offset = jax.random.randint(k_offset, (P_SIZE,), 0, spacing).astype(jnp.int32)
    return (slots // PMAX * ROWS_DEV + slots % PMAX * spacing + offset).astype(jnp.int32)


def place_ends(values, stream_key, least, high):
    longest = values.shape.index(max(values.shape))
    spots = []
    for shift in (0, 1):
        where = [jax.random.randint(jax.random.fold_in(stream_key, axis), (), 0, length) for axis, length in enumerate(values.shape)]
        where[longest] = (where[longest] + shift) % values.shape[longest]
        spots.append(tuple(where))
    return values.at[spots[0]].set(least).at[spots[1]].set(high)


def setup_inputs(seed: int = 0) -> dict:
    key_list = jax.random.split(jax.random.key(seed), 5)
    return {
        "embeddings": draw_embeddings(jax.random.fold_in(key_list[4], 71), 0),
        "factor_cols": draw_factor_cols(jax.random.fold_in(key_list[4], 71), 0),
        "solved": place_ends(jax.random.randint(key_list[2], (NUM_ROWS,), 0, 17), jax.random.fold_in(key_list[2], 1), 0, 16).astype(jnp.int32),
        "pivots": draw_pivots(jax.random.fold_in(key_list[4], 71), 0),
    }


EPS = 1e-06
TAU = 6.0
RIDGE = 1.0

def learn(counts):
    c = counts.astype(jnp.float32)
    return (c * (16.0 - c) + 8.0) / 72.0

def scales(emb):
    x = emb.astype(jnp.float32)
    return jnp.sqrt(lax.optimization_barrier(jnp.mean(x * x, axis=1)) + EPS)

def kernel_panel(left_emb, left_fac, left_q, left_norm, left_ids, piv_emb, piv_fac, piv_q, piv_norm, pivots):
    dims = (((1,), (1,)), ((), ()))
    dots = lax.dot_general(left_emb.astype(jnp.float32), piv_emb.astype(jnp.float32), dims, preferred_element_type=jnp.float32)
    width = left_emb.shape[1] * 1.0
    cosine = dots / (width * left_norm[:, None] * piv_norm[None, :])
    similar = jnp.exp(TAU * (cosine - 1.0))
    ridge = jnp.where(left_ids[:, None] == pivots[None, :], RIDGE, 0.0)
    shared = lax.dot_general(left_fac.astype(jnp.float32), piv_fac.astype(jnp.float32), dims, preferred_element_type=jnp.float32)
    return left_q[:, None] * piv_q[None, :] * similar + ridge - shared

def reference(embeddings, factor_cols, solved, pivots):
    piv_emb = embeddings[pivots]
    piv_fac = factor_cols[pivots]
    piv_q = learn(solved[pivots])
    piv_norm = scales(piv_emb)
    block = kernel_panel(piv_emb, piv_fac, piv_q, piv_norm, pivots, piv_emb, piv_fac, piv_q, piv_norm, pivots)
    lower = jnp.linalg.cholesky(block)
    blocks = embeddings.shape[0] // ROWS_DEV

    def one(index):
        start = index * ROWS_DEV
        emb = lax.dynamic_slice_in_dim(embeddings, start, ROWS_DEV, 0)
        fac = lax.dynamic_slice_in_dim(factor_cols, start, ROWS_DEV, 0)
        counts = lax.dynamic_slice_in_dim(solved, start, ROWS_DEV, 0)
        row_q = learn(counts)
        row_ids = start + jnp.arange(ROWS_DEV, dtype=jnp.int32)
        panel = kernel_panel(emb, fac, row_q, scales(emb), row_ids, piv_emb, piv_fac, piv_q, piv_norm, pivots)
        full = jax.scipy.linalg.solve_triangular(lower, panel.T, lower=True).T
        facf = fac.astype(jnp.float32)
        gain = row_q * row_q + RIDGE - lax.optimization_barrier(jnp.sum(facf * facf, axis=1)) - lax.optimization_barrier(jnp.sum(full * full, axis=1))
        return (full.astype(jnp.bfloat16), gain)
    new_cols, gains = lax.map(one, jnp.arange(blocks, dtype=jnp.int32))
    new_cols = new_cols.reshape(blocks * ROWS_DEV, pivots.shape[0])
    gains = gains.reshape(blocks * ROWS_DEV)
    return (new_cols, gains, jnp.max(gains))
```

```python
import functools

import jax
import jax.numpy as jnp
from jax import lax
from jax.experimental import pallas as pl
from jax.experimental.pallas import tpu as pltpu
from jax.sharding import PartitionSpec as P

PMAX = 16
EPS = 1e-06
TAU = 6.0
RIDGE = 1.0
AXES = ("rows", "cols")
NDEV = 128
TILES = 8
BS = 32
F32 = jnp.float32
BF16 = jnp.bfloat16


def iota(shape, dim):
    return lax.broadcasted_iota(jnp.int32, shape, dim)


def learn(c):
    return (c * (16.0 - c) + 8.0) / 72.0


def gather_kernel(dev_ref, piv_s, piv_v, solved_ref, emb_ref, fac_ref, out_ref, ebuf, fbuf, sem):
    rows_here = emb_ref.shape[0]
    total = piv_s.shape[0]
    dim = emb_ref.shape[1]
    first = dev_ref[0] * rows_here
    pv = piv_v[...]
    before = jnp.sum((pv < first).astype(F32)).astype(jnp.int32)
    upto = jnp.sum((pv < first + rows_here).astype(F32)).astype(jnp.int32)
    mine = upto - before
    idx = []
    copies = []
    for s in range(PMAX):
        p = piv_s[jnp.minimum(before + s, total - 1)]
        i = jnp.clip(p - first, 0, rows_here - 1)
        idx.append(i)
        base = pl.multiple_of((i // 16) * 16, 16)
        c1 = pltpu.make_async_copy(
            emb_ref.at[pl.ds(base, 16), :], ebuf.at[pl.ds(16 * s, 16), :], sem.at[0, s]
        )
        c2 = pltpu.make_async_copy(
            fac_ref.at[pl.ds(base, 16), :], fbuf.at[pl.ds(16 * s, 16), :], sem.at[1, s]
        )
        c1.start()
        c2.start()
        copies += [c1, c2]
    r = iota((NDEV, 16 * PMAX), 0)
    q = iota((NDEV, 16 * PMAX), 1)
    rc = iota((NDEV, 128), 0)
    hot = jnp.zeros((NDEV, 16 * PMAX), F32)
    cnt = jnp.zeros((NDEV, 128), F32)
    for s in range(PMAX):
        home = jnp.where(s < mine, lax.rem(before + s, NDEV), -1)
        col = 16 * s + lax.rem(idx[s], 16)
        hot = jnp.where((r == home) & (q == col), 1.0, hot)
        c = solved_ref[idx[s] // 128, lax.rem(idx[s], 128)].astype(F32)
        cnt = jnp.where(rc == home, c, cnt)
    hot = hot.astype(BF16)
    for c in copies:
        c.wait()
    out_ref[:, 0:dim] = jnp.dot(hot, ebuf[...], preferred_element_type=F32).astype(BF16)
    out_ref[:, dim : dim + fbuf.shape[1]] = jnp.dot(
        hot, fbuf[...], preferred_element_type=F32
    ).astype(BF16)
    out_ref[:, dim + fbuf.shape[1] :] = cnt.astype(BF16)


def split3(x):
    h = x.astype(BF16)
    r = x - h.astype(F32)
    m = r.astype(BF16)
    l = (r - m.astype(F32)).astype(BF16)
    return h, m, l


def main_kernel(
    dev_ref, piv_ref, recv_ref, solved_ref, emb_ref, fac_ref,
    out_ref, gains_ref, best_ref,
    pivt, pvec, ar, minv, mt, panel, base,
):
    i = pl.program_id(0)
    tile = emb_ref.shape[0]
    dim = emb_ref.shape[1]
    k0 = fac_ref.shape[1]
    n = recv_ref.shape[0]
    half = n // 2
    nchunk = tile // 128
    tdims = (((0,), (0,)), ((), ()))

    @pl.when(i == 0)
    def _():
        jj = iota((n, n), 0)
        qq = iota((n, n), 1)
        perm = (qq == 2 * lax.rem(jj, half) + jj // half).astype(BF16)
        piv = jnp.dot(perm, recv_ref[...], preferred_element_type=F32)
        pt = piv.T
        pivt[...] = pt[0 : dim + k0, :].astype(BF16)
        ps = jnp.sqrt(jnp.sum(pt[0:dim, :] * pt[0:dim, :], axis=0, keepdims=True) / dim + EPS)
        pq = learn(pt[dim + k0 : dim + k0 + 1, :])
        pvec[0:1, :] = TAU / (dim * ps)
        pvec[1:2, :] = pq
        cs = jnp.sqrt(jnp.sum(piv[:, 0:dim] * piv[:, 0:dim], axis=1, keepdims=True) / dim + EPS)
        cq = learn(piv[:, dim + k0 : dim + k0 + 1])
        pb = piv.astype(BF16)
        dots = jnp.dot(pb[:, 0:dim], pivt[0:dim, :], preferred_element_type=F32)
        shared = jnp.dot(pb[:, dim : dim + k0], pivt[dim : dim + k0, :], preferred_element_type=F32)
        similar = jnp.exp(dots * (1.0 / cs) * pvec[0:1, :] - TAU)
        eye = (jj == qq).astype(F32)
        ar[:, 0:n] = similar * cq * pq + RIDGE * eye - shared
        ar[:, n : 2 * n] = eye

    @pl.when(i < TILES)
    def _():
        x = emb_ref[...]
        f = fac_ref[...]
        xf = x.astype(F32)
        ff = f.astype(F32)
        rs = jnp.sqrt(jnp.sum(xf * xf, axis=1, keepdims=True) / dim + EPS)
        fs = jnp.sum(ff * ff, axis=1, keepdims=True)
        st = solved_ref[pl.ds(i * nchunk, nchunk), :].astype(F32)
        ey = iota((128, 128), 0) == iota((128, 128), 1)
        cols = []
        for c in range(nchunk):
            b = jnp.broadcast_to(st[c : c + 1, :], (128, 128))
            cols.append(jnp.sum(jnp.where(ey, b, 0.0), axis=1, keepdims=True))
        q = learn(jnp.concatenate(cols, axis=0))
        base[pl.ds(pl.multiple_of(i * tile, tile), tile), :] = jnp.broadcast_to(
            q * q + RIDGE - fs, (tile, 128)
        )
        dots = jnp.dot(x, pivt[0:dim, :], preferred_element_type=F32)
        shared = jnp.dot(f, pivt[dim : dim + k0, :], preferred_element_type=F32)
        similar = jnp.exp(dots * (1.0 / rs) * pvec[0:1, :] - TAU)
        ids = dev_ref[0] * (tile * TILES) + i * tile + iota((tile, n), 0)
        ridge = jnp.where(ids == piv_ref[...], RIDGE, 0.0)
        p = similar * (q * pvec[1:2, :]) + ridge - shared
        ph = p.astype(BF16)
        plo = (p - ph.astype(F32)).astype(BF16)
        o = pl.ds(pl.multiple_of(i * tile, tile), tile)
        panel[o, 0:n] = ph
        panel[o, n : 2 * n] = plo

        rows = pl.ds(pl.multiple_of(i * BS, BS), BS)
        shift = lax.rem(n - i * BS, n)
        a = pltpu.roll(ar[rows, 0:n], shift, 1)
        w = jnp.concatenate([a, ar[rows, n : 2 * n]], axis=1)
        groups = [w[8 * g : 8 * g + 8, :] for g in range(BS // 8)]
        sub = iota((8, 1), 0)
        for k in range(BS):
            g0 = k // 8
            row = groups[g0][k % 8 : k % 8 + 1, :]
            inv = 1.0 / row[:, k : k + 1]
            srow = row * inv
            for g in range(g0, BS // 8):
                col = groups[g][:, k : k + 1]
                if g == g0:
                    if k % 8 == 7:
                        continue
                    col = jnp.where(sub > k % 8, col, 0.0)
                groups[g] = groups[g] - col * srow
        w = jnp.concatenate(groups, axis=0)
        d = jnp.sum(
            jnp.where(iota((BS, 128), 0) == iota((BS, 128), 1), w[:, 0:128], 0.0),
            axis=1, keepdims=True,
        )
        w = w * (1.0 / jnp.sqrt(d))
        u = pltpu.roll(w[:, 0:n], i * BS, 1)
        m = w[:, n : 2 * n]
        minv[rows, :] = m
        uh, um, ul = split3(u)
        mh, mm, ml = split3(m)
        left = jnp.concatenate([uh, uh, um, uh, ul, um], axis=0)
        r_a = jnp.concatenate([uh, um, uh, ul, uh, um], axis=0)
        r_m = jnp.concatenate([mh, mm, mh, ml, mh, mm], axis=0)
        ar[:, 0:n] -= lax.dot_general(left, r_a, tdims, preferred_element_type=F32)
        ar[:, n : 2 * n] -= lax.dot_general(left, r_m, tdims, preferred_element_type=F32)

    @pl.when(i == TILES)
    def _():
        t = minv[...].T
        h = t.astype(BF16)
        mt[0:n, :] = h
        mt[n : 2 * n, :] = h
        mt[2 * n : 3 * n, :] = (t - h.astype(F32)).astype(BF16)
        best_ref[...] = jnp.full(best_ref.shape, -jnp.inf, F32)

    @pl.when(i >= TILES)
    def _():
        t = i - TILES
        o = pl.ds(pl.multiple_of(t * tile, tile), tile)
        full = jnp.dot(panel[o, :], mt[0 : 2 * n, :], preferred_element_type=F32)
        full += jnp.dot(panel[o, 0:n], mt[2 * n : 3 * n, :], preferred_element_type=F32)
        out_ref[...] = full.astype(BF16)
        g = base[o, :] - jnp.sum(full * full, axis=1, keepdims=True)
        ey = iota((128, 128), 0) == iota((128, 128), 1)
        lines = []
        for c in range(nchunk):
            lines.append(
                jnp.sum(jnp.where(ey, g[128 * c : 128 * c + 128, :], 0.0), axis=0, keepdims=True)
            )
        gains_ref[pl.ds(t * nchunk, nchunk), :] = jnp.concatenate(lines, axis=0)
        best_ref[...] = jnp.maximum(best_ref[...], jnp.max(g))


def body(embeddings, factor_cols, solved, pivots):
    rows_here, dim = embeddings.shape
    k0 = factor_cols.shape[1]
    total = pivots.shape[0]
    width = dim + k0 + 128
    tile = rows_here // TILES
    device = lax.axis_index(AXES).astype(jnp.int32)
    dev = device.reshape(1)
    solved2 = solved.reshape(rows_here // 128, 128)
    piv2 = pivots.reshape(total // 128, 128)
    smem = pl.BlockSpec(memory_space=pltpu.SMEM)
    vmem = pl.BlockSpec(memory_space=pltpu.VMEM)
    hbm = pl.BlockSpec(memory_space=pl.ANY)
    send = pl.pallas_call(
        gather_kernel,
        out_shape=jax.ShapeDtypeStruct((NDEV, width), BF16),
        in_specs=[smem, smem, vmem, smem, hbm, hbm],
        out_specs=vmem,
        scratch_shapes=[
            pltpu.VMEM((16 * PMAX, dim), BF16),
            pltpu.VMEM((16 * PMAX, k0), BF16),
            pltpu.SemaphoreType.DMA((2, PMAX)),
        ],
        compiler_params=pltpu.CompilerParams(vmem_limit_bytes=8 << 20),
        name="own_rows",
    )(dev, pivots, piv2, solved2, embeddings, factor_cols)
    got = lax.all_to_all(send.reshape(NDEV, 1, width), AXES, 0, 0)
    owner = pivots // rows_here
    pair = [
        lax.dynamic_slice(got, (owner[device + NDEV * t], 0, 0), (1, 1, width))
        for t in range(total // NDEV)
    ]
    pair = jnp.concatenate(pair, axis=1)
    recv = lax.all_to_all(
        jnp.broadcast_to(pair, (NDEV, total // NDEV, width)), AXES, 0, 0
    ).reshape(total, width)
    new_cols, gains, best = pl.pallas_call(
        main_kernel,
        grid=(2 * TILES,),
        out_shape=(
            jax.ShapeDtypeStruct((rows_here, total), BF16),
            jax.ShapeDtypeStruct((rows_here // 128, 128), F32),
            jax.ShapeDtypeStruct((NDEV, 128), F32),
        ),
        in_specs=[
            smem, vmem, vmem, vmem,
            pl.BlockSpec((tile, dim), lambda i: (jnp.minimum(i, TILES - 1), 0)),
            pl.BlockSpec((tile, k0), lambda i: (jnp.minimum(i, TILES - 1), 0)),
        ],
        out_specs=(
            pl.BlockSpec((tile, total), lambda i: (jnp.maximum(i - TILES, 0), 0)),
            pl.BlockSpec((rows_here // 128, 128), lambda i: (0, 0)),
            pl.BlockSpec((NDEV, 128), lambda i: (0, 0)),
        ),
        scratch_shapes=[
            pltpu.VMEM((dim + k0, total), BF16),
            pltpu.VMEM((8, total), F32),
            pltpu.VMEM((total, 2 * total), F32),
            pltpu.VMEM((total, total), F32),
            pltpu.VMEM((3 * total, total), BF16),
            pltpu.VMEM((rows_here, 2 * total), BF16),
            pltpu.VMEM((rows_here, 128), F32),
        ],
        compiler_params=pltpu.CompilerParams(
            dimension_semantics=("arbitrary",), vmem_limit_bytes=48 << 20
        ),
        name="panel_factor",
    )(dev, pivots.reshape(1, total), recv, solved2, embeddings, factor_cols)
    peers = lax.all_to_all(best.reshape(NDEV, 1, 128), AXES, 0, 0)
    return new_cols, gains.reshape(rows_here), jnp.max(peers)


def solution(mesh):
    in_specs = (P(AXES, None), P(AXES, None), P(AXES), P())
    out_specs = (P(AXES, None), P(AXES), P())
    return jax.shard_map(body, mesh=mesh, in_specs=in_specs, out_specs=out_specs, check_vma=False)
```

```python
import functools

import jax
import jax.numpy as jnp
from jax import lax
from jax.experimental import pallas as pl
from jax.experimental.pallas import tpu as pltpu
from jax.sharding import PartitionSpec as P

PMAX = 16
EPS = 1e-06
TAU = 6.0
RIDGE = 1.0
AXES = ("rows", "cols")
NDEV = 128
CLASSES = 8
RING = 4
SUB = 4
LOG2E = 1.4426950408889634
TILES = 8
BS = 32
F32 = jnp.float32
BF16 = jnp.bfloat16


def iota(shape, dim):
    return lax.broadcasted_iota(jnp.int32, shape, dim)


def learn(c):
    return (c * (16.0 - c) + 8.0) / 72.0


def own_kernel(
    pos_ref, piv_s, piv_v, solved_ref, emb_ref, fac_ref, keep_ref, send_ref, loc_ref, ebuf, fbuf, sem
):
    rows_here, dim = emb_ref.shape
    k0 = fac_ref.shape[1]
    total = piv_s.shape[0]
    first = pos_ref[0] * rows_here
    z = pos_ref[1]
    core = pos_ref[2]
    pv = piv_v[...]
    before = jnp.sum((pv < first).astype(F32)).astype(jnp.int32)
    upto = jnp.sum((pv < first + rows_here).astype(F32)).astype(jnp.int32)
    mine = upto - before
    loc_ref[0] = before
    loc_ref[1] = mine
    idx = []
    copies = []
    for s in range(PMAX):
        p = piv_s[jnp.minimum(before + s, total - 1)]
        i = jnp.clip(p - first, 0, rows_here - 1)
        loc_ref[2 + s] = i
        idx.append(i)
        base = pl.multiple_of((i // 16) * 16, 16)
        c1 = pltpu.make_async_copy(
            emb_ref.at[pl.ds(base, 16), :], ebuf.at[pl.ds(16 * s, 16), :], sem.at[0, s]
        )
        c2 = pltpu.make_async_copy(
            fac_ref.at[pl.ds(base, 16), :], fbuf.at[pl.ds(16 * s, 16), :], sem.at[1, s]
        )
        c1.start()
        c2.start()
        copies += [c1, c2]
    r = iota((16, 16 * PMAX), 0)
    q = iota((16, 16 * PMAX), 1)
    rc = iota((16, 128), 0)
    lane = iota((16, 128), 1)
    hot = jnp.zeros((16, 16 * PMAX), F32)
    tag = jnp.zeros((16, 128), F32)
    for s in range(PMAX):
        j = before + s
        cls = lax.rem(j, CLASSES)
        row = 2 * jnp.bitwise_xor(cls // 2, z) + s // CLASSES
        row = row + jnp.where(lax.rem(cls, 2) == core, 0, 8)
        row = jnp.where(s < mine, row, -1)
        hot = jnp.where((r == row) & (q == 16 * s + lax.rem(idx[s], 16)), 1.0, hot)
        c = solved_ref[idx[s] // 128, lax.rem(idx[s], 128)].astype(F32)
        tag = jnp.where(rc == row, jnp.where(lane == 0, c, (j + 1).astype(F32)), tag)
    hot = hot.astype(BF16)
    for c in copies:
        c.wait()
    e = jnp.dot(hot, ebuf[...], preferred_element_type=F32).astype(BF16)
    f = jnp.dot(hot, fbuf[...], preferred_element_type=F32).astype(BF16)
    t = tag.astype(BF16)
    for o, ref in ((0, keep_ref), (8, send_ref)):
        ref[:, 0:dim] = e[o : o + 8, :]
        ref[:, dim : dim + k0] = f[o : o + 8, :]
        ref[:, dim + k0 :] = t[o : o + 8, :]


def split_kernel(keep_ref, recv_ref, *outs):
    both = jnp.concatenate([keep_ref[...], recv_ref[...]], axis=0)
    r = iota((8, 16), 0)
    q = iota((8, 16), 1)
    for k, out in enumerate(outs):
        want = jnp.where(r < 2, 2 * k + r, 8 + 2 * k + r - 2)
        hot = ((q == want) & (r < 4)).astype(BF16)
        out[...] = jnp.dot(hot, both, preferred_element_type=F32).astype(BF16)


def pack_kernel(*refs):
    out = refs[-1]
    data = jnp.concatenate([ref[...] for ref in refs[:-1]], axis=0)
    r = iota((16, 32), 0)
    q = iota((16, 32), 1)
    hot = (q == 8 * (r // 4) + lax.rem(r, 4)).astype(BF16)
    out[...] = jnp.dot(hot, data, preferred_element_type=F32).astype(BF16)


def slots_kernel(cls_ref, *refs):
    out = refs[-1]
    slots, width = out.shape
    data = jnp.concatenate([ref[...] for ref in refs[:-1]], axis=0)
    ids = data[:, width - 127 : width - 126].astype(F32)
    want = (CLASSES * iota((data.shape[0], slots), 1) + cls_ref[0] + 1).astype(F32)
    hot = (ids == want).astype(BF16)
    out[...] = lax.dot_general(
        hot, data, (((0,), (0,)), ((), ())), preferred_element_type=F32
    ).astype(BF16)


def norms_kernel(solved_ref, emb_ref, fac_ref, aux_ref):
    i = pl.program_id(0)
    tile, dim = emb_ref.shape
    nchunk = tile // 128
    st = solved_ref[pl.ds(i * nchunk, nchunk), :].astype(F32)
    ey = iota((128, 128), 0) == iota((128, 128), 1)
    lane = iota((128, 128), 1)
    for c in range(nchunk):
        o = slice(128 * c, 128 * c + 128)
        x = emb_ref[o, :].astype(F32)
        f = fac_ref[o, :].astype(F32)
        a = 1.0 / jnp.sqrt(jnp.sum(x * x, axis=1, keepdims=True) / dim + EPS)
        fs = jnp.sum(f * f, axis=1, keepdims=True)
        b = jnp.broadcast_to(st[c : c + 1, :], (128, 128))
        q = learn(jnp.sum(jnp.where(ey, b, 0.0), axis=1, keepdims=True))
        aux_ref[o, :] = jnp.where(lane == 0, a, jnp.where(lane == 1, q, q * q + RIDGE - fs))

def split3(x):
    h = x.astype(BF16)
    r = x - h.astype(F32)
    m = r.astype(BF16)
    l = (r - m.astype(F32)).astype(BF16)
    return h, m, l


def main_kernel(
    loc_ref, one_ref, two_ref, aux_ref, emb_ref, fac_ref,
    out_ref, gains_ref, best_ref,
    piv, pvec, ar, minv, mt, panel, base,
):
    i = pl.program_id(0)
    tile, dim = emb_ref.shape
    k0 = fac_ref.shape[1]
    n = piv.shape[0]
    nchunk = tile // 128
    sub = tile // SUB
    tdims = (((0,), (0,)), ((), ()))
    ndims = (((1,), (1,)), ((), ()))

    @pl.when(i == 0)
    def _():
        jj = iota((n, n), 0)
        qq = iota((n, n), 1)
        eye = (jj == qq).astype(F32)
        data = jnp.concatenate([one_ref[...], two_ref[...]], axis=0)
        ids = data[:, dim + k0 + 1 : dim + k0 + 2].astype(F32)
        permt = (ids == (qq + 1).astype(F32)).astype(BF16)
        v = lax.dot_general(permt, data, tdims, preferred_element_type=F32)
        pb = v.astype(BF16)
        piv[...] = pb[:, 0 : dim + k0]
        cs = 1.0 / jnp.sqrt(
            jnp.sum(v[:, 0:dim] * v[:, 0:dim], axis=1, keepdims=True) / dim + EPS
        )
        cq = learn(v[:, dim + k0 : dim + k0 + 1])
        rs = jnp.sum(eye * cs, axis=0, keepdims=True) * (TAU * LOG2E / dim)
        rq = jnp.sum(eye * cq, axis=0, keepdims=True)
        pvec[0:1, :] = rs
        pvec[1:2, :] = rq
        dots = lax.dot_general(pb[:, 0:dim], piv[:, 0:dim], ndims, preferred_element_type=F32)
        shared = lax.dot_general(
            pb[:, dim : dim + k0], piv[:, dim : dim + k0], ndims, preferred_element_type=F32
        )
        similar = jnp.exp2(dots * (cs * rs) - TAU * LOG2E)
        ar[:, 0:n] = similar * (cq * rq) + RIDGE * eye - shared
        ar[:, n : 2 * n] = eye

    @pl.when(i < TILES)
    def _():
        for c in range(SUB):
            o = slice(sub * c, sub * c + sub)
            a = aux_ref[o, 0:1]
            q = aux_ref[o, 1:2]
            dots = lax.dot_general(
                emb_ref[o, :], piv[:, 0:dim], ndims, preferred_element_type=F32
            )
            shared = lax.dot_general(
                fac_ref[o, :], piv[:, dim : dim + k0], ndims, preferred_element_type=F32
            )
            similar = jnp.exp2(dots * (a * pvec[0:1, :]) - TAU * LOG2E)
            p = similar * (q * pvec[1:2, :]) - shared
            ph = p.astype(BF16)
            w = pl.ds(pl.multiple_of(i * tile + sub * c, 16), sub)
            panel[w, 0:n] = ph
            panel[w, n : 2 * n] = (p - ph.astype(F32)).astype(BF16)
            base[w, :] = jnp.broadcast_to(aux_ref[o, 2:3], (sub, 128))

        rows = pl.ds(pl.multiple_of(i * BS, BS), BS)
        shift = lax.rem(n - i * BS, n)
        a = pltpu.roll(ar[rows, 0:n], shift, 1)
        w = jnp.concatenate([a, ar[rows, n : 2 * n]], axis=1)
        groups = [w[8 * g : 8 * g + 8, :] for g in range(BS // 8)]
        srows = iota((8, 1), 0)
        for k in range(BS):
            g0 = k // 8
            row = groups[g0][k % 8 : k % 8 + 1, :]
            srow = row * (1.0 / row[:, k : k + 1])
            for g in range(g0, BS // 8):
                col = groups[g][:, k : k + 1]
                if g == g0:
                    if k % 8 == 7:
                        continue
                    col = jnp.where(srows > k % 8, col, 0.0)
                groups[g] = groups[g] - col * srow
        w = jnp.concatenate(groups, axis=0)
        d = jnp.sum(
            jnp.where(iota((BS, 128), 0) == iota((BS, 128), 1), w[:, 0:128], 0.0),
            axis=1, keepdims=True,
        )
        w = w * (1.0 / jnp.sqrt(d))
        u = pltpu.roll(w[:, 0:n], i * BS, 1)
        m = w[:, n : 2 * n]
        minv[rows, :] = m
        uh, um, ul = split3(u)
        mh, mm, ml = split3(m)
        left = jnp.concatenate([uh, uh, um, uh, ul, um], axis=0)
        r_a = jnp.concatenate([uh, um, uh, ul, uh, um], axis=0)
        r_m = jnp.concatenate([mh, mm, mh, ml, mh, mm], axis=0)
        ar[:, 0:n] -= lax.dot_general(left, r_a, tdims, preferred_element_type=F32)
        ar[:, n : 2 * n] -= lax.dot_general(left, r_m, tdims, preferred_element_type=F32)

    @pl.when(i == TILES)
    def _():
        t = minv[...].T
        h = t.astype(BF16)
        mt[0:n, :] = h
        mt[n : 2 * n, :] = h
        mt[2 * n : 3 * n, :] = (t - h.astype(F32)).astype(BF16)
        best_ref[...] = jnp.full(best_ref.shape, -jnp.inf, F32)

        def ridge(s, carry):
            at = loc_ref[2 + s]
            w = pl.ds(pl.multiple_of((at // 16) * 16, 16), 16)
            p = panel[w, 0:n].astype(F32) + panel[w, n : 2 * n].astype(F32)
            here = (iota((16, n), 0) == lax.rem(at, 16)) & (iota((16, n), 1) == loc_ref[0] + s)
            p = p + jnp.where(here, RIDGE, 0.0)
            ph = p.astype(BF16)
            panel[w, 0:n] = ph
            panel[w, n : 2 * n] = (p - ph.astype(F32)).astype(BF16)
            return carry

        lax.fori_loop(0, jnp.minimum(loc_ref[1], PMAX), ridge, 0)

    @pl.when(i >= TILES)
    def _():
        t = i - TILES
        gs = []
        for c in range(SUB):
            o = slice(sub * c, sub * c + sub)
            w = pl.ds(pl.multiple_of(t * tile + sub * c, 16), sub)
            full = jnp.dot(panel[w, :], mt[0 : 2 * n, :], preferred_element_type=F32)
            full += jnp.dot(panel[w, 0:n], mt[2 * n : 3 * n, :], preferred_element_type=F32)
            out_ref[o, :] = full.astype(BF16)
            gs.append(base[w, :] - jnp.sum(full * full, axis=1, keepdims=True))
        g = jnp.concatenate(gs, axis=0)
        ey = iota((128, 128), 0) == iota((128, 128), 1)
        lines = []
        for c in range(nchunk):
            lines.append(
                jnp.sum(jnp.where(ey, g[128 * c : 128 * c + 128, :], 0.0), axis=0, keepdims=True)
            )
        lines = jnp.concatenate(lines, axis=0)
        gains_ref[pl.ds(t * nchunk, nchunk), :] = lines
        best_ref[...] = jnp.maximum(best_ref[...], jnp.max(lines))


def ring(values, axis, pairs):
    return [lax.ppermute(v, axis, p) for v, p in zip(values, pairs)]


def body(embeddings, factor_cols, solved, pivots):
    rows_here, dim = embeddings.shape
    k0 = factor_cols.shape[1]
    total = pivots.shape[0]
    width = dim + k0 + 128
    tile = rows_here // TILES
    r = lax.axis_index("rows").astype(jnp.int32)
    c = lax.axis_index("cols").astype(jnp.int32)
    pos = jnp.stack([r * 16 + c, r // 2, r % 2])
    solved2 = solved.reshape(rows_here // 128, 128)
    piv2 = pivots.reshape(total // 128, 128)
    smem = pl.BlockSpec(memory_space=pltpu.SMEM)
    vmem = pl.BlockSpec(memory_space=pltpu.VMEM)
    hbm = pl.BlockSpec(memory_space=pltpu.HBM)
    small = pltpu.CompilerParams(vmem_limit_bytes=8 << 20)
    wide = lambda rows: jax.ShapeDtypeStruct((rows, width), BF16)
    swap = [(i, i ^ 1) for i in range(8)]
    zs = [[(i, i ^ (2 * k)) for i in range(8)] for k in range(1, RING)]
    xs = [[(i, i ^ (4 * k)) for i in range(16)] for k in range(1, RING)]
    ys = [[(i, i ^ k) for i in range(16)] for k in range(1, RING)]

    keep, send, loc = pl.pallas_call(
        own_kernel,
        out_shape=(wide(8), wide(8), jax.ShapeDtypeStruct((2 + PMAX,), jnp.int32)),
        in_specs=[smem, smem, vmem, smem, hbm, hbm],
        out_specs=(vmem, vmem, smem),
        scratch_shapes=[
            pltpu.VMEM((16 * PMAX, dim), BF16),
            pltpu.VMEM((16 * PMAX, k0), BF16),
            pltpu.SemaphoreType.DMA((2, PMAX)),
        ],
        compiler_params=small,
        name="own_rows",
    )(pos, pivots, piv2, solved2, embeddings, factor_cols)
    aux = pl.pallas_call(
        norms_kernel,
        grid=(TILES,),
        out_shape=jax.ShapeDtypeStruct((rows_here, 128), F32),
        in_specs=[
            vmem,
            pl.BlockSpec((tile, dim), lambda i: (i, 0)),
            pl.BlockSpec((tile, k0), lambda i: (i, 0)),
        ],
        out_specs=pl.BlockSpec((tile, 128), lambda i: (i, 0)),
        compiler_params=pltpu.CompilerParams(
            dimension_semantics=("arbitrary",), vmem_limit_bytes=40 << 20
        ),
        cost_estimate=pl.CostEstimate(
            flops=rows_here * (dim + k0) * 4, bytes_accessed=rows_here * (dim + k0) * 2,
            transcendentals=0,
        ),
        name="row_norms",
    )(solved2, embeddings, factor_cols)
    recv = lax.ppermute(send, "rows", swap)
    parts = pl.pallas_call(
        split_kernel, out_shape=(wide(8),) * RING, compiler_params=small, name="by_class",
    )(keep, recv)
    got = [parts[0]] + ring(parts[1:], "rows", zs)
    mine = pl.pallas_call(
        pack_kernel, out_shape=wide(16), compiler_params=small, name="pack",
    )(*got)
    got = [mine] + ring([mine] * 3, "cols", xs)
    mine = pl.pallas_call(
        slots_kernel,
        out_shape=wide(total // CLASSES),
        in_specs=[smem] + [vmem] * RING,
        out_specs=vmem,
        compiler_params=small,
        name="slots",
    )(r.reshape(1), *got)
    got = [mine] + ring([mine] * 3, "cols", ys)
    mine = got[0] + got[1] + got[2] + got[3]
    got = [mine] + ring([mine] * 3, "rows", zs)
    one = jnp.concatenate(got, axis=0)
    two = lax.ppermute(one, "rows", swap)

    new_cols, gains, best = pl.pallas_call(
        main_kernel,
        grid=(2 * TILES,),
        out_shape=(
            jax.ShapeDtypeStruct((rows_here, total), BF16),
            jax.ShapeDtypeStruct((rows_here // 128, 128), F32),
            jax.ShapeDtypeStruct((NDEV, 128), F32),
        ),
        in_specs=[
            smem, vmem, vmem,
            pl.BlockSpec((tile, 128), lambda i: (jnp.minimum(i, TILES - 1), 0)),
            pl.BlockSpec((tile, dim), lambda i: (jnp.minimum(i, TILES - 1), 0)),
            pl.BlockSpec((tile, k0), lambda i: (jnp.minimum(i, TILES - 1), 0)),
        ],
        out_specs=(
            pl.BlockSpec((tile, total), lambda i: (jnp.maximum(i - TILES, 0), 0)),
            pl.BlockSpec((rows_here // 128, 128), lambda i: (0, 0)),
            pl.BlockSpec((NDEV, 128), lambda i: (0, 0)),
        ),
        scratch_shapes=[
            pltpu.VMEM((total, dim + k0), BF16),
            pltpu.VMEM((8, total), F32),
            pltpu.VMEM((total, 2 * total), F32),
            pltpu.VMEM((total, total), F32),
            pltpu.VMEM((3 * total, total), BF16),
            pltpu.VMEM((rows_here, 2 * total), BF16),
            pltpu.VMEM((rows_here, 128), F32),
        ],
        compiler_params=pltpu.CompilerParams(
            dimension_semantics=("arbitrary",), vmem_limit_bytes=48 << 20
        ),
        name="panel_factor",
    )(loc, one, two, aux, embeddings, factor_cols)
    peers = lax.all_to_all(best.reshape(NDEV, 1, 128), AXES, 0, 0)
    return new_cols, gains.reshape(rows_here), jnp.max(peers)


def solution(mesh):
    in_specs = (P(AXES, None), P(AXES, None), P(AXES), P())
    out_specs = (P(AXES, None), P(AXES), P())
    return jax.shard_map(body, mesh=mesh, in_specs=in_specs, out_specs=out_specs, check_vma=False)
```

```python
import functools

import jax
import jax.numpy as jnp
from jax import lax
from jax.experimental import pallas as pl
from jax.experimental.pallas import tpu as pltpu
from jax.sharding import PartitionSpec as P

PMAX = 16
EPS = 1e-06
TAU = 6.0
RIDGE = 1.0
AXES = ("rows", "cols")
NDEV = 128
CLASSES = 8
RING = 4
SUB = 4
GRANT = 58 << 20
LOG2E = 1.4426950408889634
TILES = 8
BS = 32
F32 = jnp.float32
BF16 = jnp.bfloat16


def iota(shape, dim):
    return lax.broadcasted_iota(jnp.int32, shape, dim)


def learn(c):
    return (c * (16.0 - c) + 8.0) / 72.0


def own_kernel(
    pos_ref, piv_s, piv_v, solved_ref, emb_ref, fac_ref, keep_ref, send_ref, loc_ref, ebuf, fbuf, sem
):
    rows_here, dim = emb_ref.shape
    k0 = fac_ref.shape[1]
    total = piv_s.shape[0]
    first = pos_ref[0] * rows_here
    z = pos_ref[1]
    core = pos_ref[2]
    pv = piv_v[...]
    before = jnp.sum((pv < first).astype(F32)).astype(jnp.int32)
    upto = jnp.sum((pv < first + rows_here).astype(F32)).astype(jnp.int32)
    mine = upto - before
    loc_ref[0] = before
    loc_ref[1] = mine
    idx = []
    copies = []
    for s in range(PMAX):
        p = piv_s[jnp.minimum(before + s, total - 1)]
        i = jnp.clip(p - first, 0, rows_here - 1)
        loc_ref[2 + s] = i
        idx.append(i)
        base = pl.multiple_of((i // 16) * 16, 16)
        c1 = pltpu.make_async_copy(
            emb_ref.at[pl.ds(base, 16), :], ebuf.at[pl.ds(16 * s, 16), :], sem.at[0, s]
        )
        c2 = pltpu.make_async_copy(
            fac_ref.at[pl.ds(base, 16), :], fbuf.at[pl.ds(16 * s, 16), :], sem.at[1, s]
        )
        c1.start()
        c2.start()
        copies += [c1, c2]
    r = iota((16, 16 * PMAX), 0)
    q = iota((16, 16 * PMAX), 1)
    rc = iota((16, 128), 0)
    lane = iota((16, 128), 1)
    hot = jnp.zeros((16, 16 * PMAX), F32)
    tag = jnp.zeros((16, 128), F32)
    for s in range(PMAX):
        j = before + s
        cls = lax.rem(j, CLASSES)
        row = 2 * jnp.bitwise_xor(cls // 2, z) + s // CLASSES
        row = row + jnp.where(lax.rem(cls, 2) == core, 0, 8)
        row = jnp.where(s < mine, row, -1)
        hot = jnp.where((r == row) & (q == 16 * s + lax.rem(idx[s], 16)), 1.0, hot)
        c = solved_ref[idx[s] // 128, lax.rem(idx[s], 128)].astype(F32)
        tag = jnp.where(rc == row, jnp.where(lane == 0, c, (j + 1).astype(F32)), tag)
    hot = hot.astype(BF16)
    for c in copies:
        c.wait()
    e = jnp.dot(hot, ebuf[...], preferred_element_type=F32).astype(BF16)
    f = jnp.dot(hot, fbuf[...], preferred_element_type=F32).astype(BF16)
    t = tag.astype(BF16)
    for o, ref in ((0, keep_ref), (8, send_ref)):
        ref[:, 0:dim] = e[o : o + 8, :]
        ref[:, dim : dim + k0] = f[o : o + 8, :]
        ref[:, dim + k0 :] = t[o : o + 8, :]


def split_kernel(keep_ref, recv_ref, *outs):
    both = jnp.concatenate([keep_ref[...], recv_ref[...]], axis=0)
    r = iota((8, 16), 0)
    q = iota((8, 16), 1)
    for k, out in enumerate(outs):
        want = jnp.where(r < 2, 2 * k + r, 8 + 2 * k + r - 2)
        hot = ((q == want) & (r < 4)).astype(BF16)
        out[...] = jnp.dot(hot, both, preferred_element_type=F32).astype(BF16)


def pack_kernel(*refs):
    out = refs[-1]
    data = jnp.concatenate([ref[...] for ref in refs[:-1]], axis=0)
    r = iota((16, 32), 0)
    q = iota((16, 32), 1)
    hot = (q == 8 * (r // 4) + lax.rem(r, 4)).astype(BF16)
    out[...] = jnp.dot(hot, data, preferred_element_type=F32).astype(BF16)


def slots_kernel(cls_ref, *refs):
    out = refs[-1]
    slots, width = out.shape
    data = jnp.concatenate([ref[...] for ref in refs[:-1]], axis=0)
    ids = data[:, width - 127 : width - 126].astype(F32)
    want = (CLASSES * iota((data.shape[0], slots), 1) + cls_ref[0] + 1).astype(F32)
    hot = (ids == want).astype(BF16)
    out[...] = lax.dot_general(
        hot, data, (((0,), (0,)), ((), ())), preferred_element_type=F32
    ).astype(BF16)


def norms_kernel(first, solved_ref, emb_ref, fac_ref, *refs):
    aux_ref = refs[-1]
    i = pl.program_id(0) + first
    tile, dim = emb_ref.shape
    nchunk = tile // 128
    st = solved_ref[pl.ds(i * nchunk, nchunk), :].astype(F32)
    ey = iota((128, 128), 0) == iota((128, 128), 1)
    lane = iota((128, 128), 1)
    for c in range(nchunk):
        o = slice(128 * c, 128 * c + 128)
        x = emb_ref[o, :].astype(F32)
        f = fac_ref[o, :].astype(F32)
        a = 1.0 / jnp.sqrt(jnp.sum(x * x, axis=1, keepdims=True) / dim + EPS)
        fs = jnp.sum(f * f, axis=1, keepdims=True)
        b = jnp.broadcast_to(st[c : c + 1, :], (128, 128))
        q = learn(jnp.sum(jnp.where(ey, b, 0.0), axis=1, keepdims=True))
        aux_ref[o, :] = jnp.where(lane == 0, a, jnp.where(lane == 1, q, q * q + RIDGE - fs))

def split3(x):
    h = x.astype(BF16)
    r = x - h.astype(F32)
    m = r.astype(BF16)
    l = (r - m.astype(F32)).astype(BF16)
    return h, m, l


def main_kernel(
    loc_ref, one_ref, two_ref, aux_ref, emb_ref, fac_ref,
    out_ref, gains_ref, best_ref,
    piv, pvec, ar, minv, mt, panel, base,
):
    i = pl.program_id(0)
    tile, dim = emb_ref.shape
    k0 = fac_ref.shape[1]
    n = piv.shape[0]
    nchunk = tile // 128
    sub = tile // SUB
    tdims = (((0,), (0,)), ((), ()))
    ndims = (((1,), (1,)), ((), ()))

    @pl.when(i == 0)
    def _():
        jj = iota((n, n), 0)
        qq = iota((n, n), 1)
        eye = (jj == qq).astype(F32)
        data = jnp.concatenate([one_ref[...], two_ref[...]], axis=0)
        ids = data[:, dim + k0 + 1 : dim + k0 + 2].astype(F32)
        permt = (ids == (qq + 1).astype(F32)).astype(BF16)
        v = lax.dot_general(permt, data, tdims, preferred_element_type=F32)
        pb = v.astype(BF16)
        piv[...] = pb[:, 0 : dim + k0]
        cs = 1.0 / jnp.sqrt(
            jnp.sum(v[:, 0:dim] * v[:, 0:dim], axis=1, keepdims=True) / dim + EPS
        )
        cq = learn(v[:, dim + k0 : dim + k0 + 1])
        rs = jnp.sum(eye * cs, axis=0, keepdims=True) * (TAU * LOG2E / dim)
        rq = jnp.sum(eye * cq, axis=0, keepdims=True)
        pvec[0:1, :] = rs
        pvec[1:2, :] = rq
        dots = lax.dot_general(pb[:, 0:dim], piv[:, 0:dim], ndims, preferred_element_type=F32)
        shared = lax.dot_general(
            pb[:, dim : dim + k0], piv[:, dim : dim + k0], ndims, preferred_element_type=F32
        )
        similar = jnp.exp2(dots * (cs * rs) - TAU * LOG2E)
        ar[:, 0:n] = similar * (cq * rq) + RIDGE * eye - shared
        ar[:, n : 2 * n] = eye

    @pl.when(i < TILES)
    def _():
        for c in range(SUB):
            o = slice(sub * c, sub * c + sub)
            a = aux_ref[o, 0:1]
            q = aux_ref[o, 1:2]
            dots = lax.dot_general(
                emb_ref[o, :], piv[:, 0:dim], ndims, preferred_element_type=F32
            )
            shared = lax.dot_general(
                fac_ref[o, :], piv[:, dim : dim + k0], ndims, preferred_element_type=F32
            )
            similar = jnp.exp2(dots * (a * pvec[0:1, :]) - TAU * LOG2E)
            p = similar * (q * pvec[1:2, :]) - shared
            ph = p.astype(BF16)
            w = pl.ds(pl.multiple_of(i * tile + sub * c, 16), sub)
            panel[w, 0:n] = ph
            panel[w, n : 2 * n] = (p - ph.astype(F32)).astype(BF16)
            base[w, :] = jnp.broadcast_to(aux_ref[o, 2:3], (sub, 128))

        rows = pl.ds(pl.multiple_of(i * BS, BS), BS)
        shift = lax.rem(n - i * BS, n)
        a = pltpu.roll(ar[rows, 0:n], shift, 1)
        w = jnp.concatenate([a, ar[rows, n : 2 * n]], axis=1)
        groups = [w[8 * g : 8 * g + 8, :] for g in range(BS // 8)]
        srows = iota((8, 1), 0)
        for k in range(BS):
            g0 = k // 8
            row = groups[g0][k % 8 : k % 8 + 1, :]
            srow = row * (1.0 / row[:, k : k + 1])
            for g in range(g0, BS // 8):
                col = groups[g][:, k : k + 1]
                if g == g0:
                    if k % 8 == 7:
                        continue
                    col = jnp.where(srows > k % 8, col, 0.0)
                groups[g] = groups[g] - col * srow
        w = jnp.concatenate(groups, axis=0)
        d = jnp.sum(
            jnp.where(iota((BS, 128), 0) == iota((BS, 128), 1), w[:, 0:128], 0.0),
            axis=1, keepdims=True,
        )
        w = w * (1.0 / jnp.sqrt(d))
        u = pltpu.roll(w[:, 0:n], i * BS, 1)
        m = w[:, n : 2 * n]
        minv[rows, :] = m
        uh, um, ul = split3(u)
        mh, mm, ml = split3(m)
        left = jnp.concatenate([uh, uh, um, uh, ul, um], axis=0)
        r_a = jnp.concatenate([uh, um, uh, ul, uh, um], axis=0)
        r_m = jnp.concatenate([mh, mm, mh, ml, mh, mm], axis=0)
        ar[:, 0:n] -= lax.dot_general(left, r_a, tdims, preferred_element_type=F32)
        ar[:, n : 2 * n] -= lax.dot_general(left, r_m, tdims, preferred_element_type=F32)

    @pl.when(i == TILES)
    def _():
        t = minv[...].T
        h = t.astype(BF16)
        mt[0:n, :] = h
        mt[n : 2 * n, :] = h
        mt[2 * n : 3 * n, :] = (t - h.astype(F32)).astype(BF16)
        best_ref[...] = jnp.full(best_ref.shape, -jnp.inf, F32)

        def ridge(s, carry):
            at = loc_ref[2 + s]
            w = pl.ds(pl.multiple_of((at // 16) * 16, 16), 16)
            p = panel[w, 0:n].astype(F32) + panel[w, n : 2 * n].astype(F32)
            here = (iota((16, n), 0) == lax.rem(at, 16)) & (iota((16, n), 1) == loc_ref[0] + s)
            p = p + jnp.where(here, RIDGE, 0.0)
            ph = p.astype(BF16)
            panel[w, 0:n] = ph
            panel[w, n : 2 * n] = (p - ph.astype(F32)).astype(BF16)
            return carry

        lax.fori_loop(0, jnp.minimum(loc_ref[1], PMAX), ridge, 0)

    @pl.when(i >= TILES)
    def _():
        t = i - TILES
        gs = []
        for c in range(SUB):
            o = slice(sub * c, sub * c + sub)
            w = pl.ds(pl.multiple_of(t * tile + sub * c, 16), sub)
            full = jnp.dot(panel[w, :], mt[0 : 2 * n, :], preferred_element_type=F32)
            full += jnp.dot(panel[w, 0:n], mt[2 * n : 3 * n, :], preferred_element_type=F32)
            out_ref[o, :] = full.astype(BF16)
            gs.append(base[w, :] - jnp.sum(full * full, axis=1, keepdims=True))
        g = jnp.concatenate(gs, axis=0)
        ey = iota((128, 128), 0) == iota((128, 128), 1)
        lines = []
        for c in range(nchunk):
            lines.append(
                jnp.sum(jnp.where(ey, g[128 * c : 128 * c + 128, :], 0.0), axis=0, keepdims=True)
            )
        lines = jnp.concatenate(lines, axis=0)
        gains_ref[pl.ds(t * nchunk, nchunk), :] = lines
        best_ref[...] = jnp.maximum(best_ref[...], jnp.max(lines))


def main_call(loc, one, two, aux, embeddings, factor_cols):
    rows_here, dim = embeddings.shape
    k0 = factor_cols.shape[1]
    total = one.shape[0] + two.shape[0]
    tile = rows_here // TILES
    smem = pl.BlockSpec(memory_space=pltpu.SMEM)
    vmem = pl.BlockSpec(memory_space=pltpu.VMEM)
    return pl.pallas_call(
        main_kernel,
        grid=(2 * TILES,),
        out_shape=(
            jax.ShapeDtypeStruct((rows_here, total), BF16),
            jax.ShapeDtypeStruct((rows_here // 128, 128), F32),
            jax.ShapeDtypeStruct((NDEV, 128), F32),
        ),
        in_specs=[
            smem, vmem, vmem,
            pl.BlockSpec((tile, 128), lambda i: (jnp.minimum(i, TILES - 1), 0)),
            pl.BlockSpec((tile, dim), lambda i: (jnp.minimum(i, TILES - 1), 0)),
            pl.BlockSpec((tile, k0), lambda i: (jnp.minimum(i, TILES - 1), 0)),
        ],
        out_specs=(
            pl.BlockSpec((tile, total), lambda i: (jnp.maximum(i - TILES, 0), 0)),
            pl.BlockSpec((rows_here // 128, 128), lambda i: (0, 0)),
            pl.BlockSpec((NDEV, 128), lambda i: (0, 0)),
        ),
        scratch_shapes=[
            pltpu.VMEM((total, dim + k0), BF16),
            pltpu.VMEM((8, total), F32),
            pltpu.VMEM((total, 2 * total), F32),
            pltpu.VMEM((total, total), F32),
            pltpu.VMEM((3 * total, total), BF16),
            pltpu.VMEM((rows_here, 2 * total), BF16),
            pltpu.VMEM((rows_here, 128), F32),
        ],
        compiler_params=pltpu.CompilerParams(
            dimension_semantics=("arbitrary",), vmem_limit_bytes=GRANT
        ),
        name="panel_factor",
    )(loc, one, two, aux, embeddings, factor_cols)


def norms_part(solved2, embeddings, factor_cols, first, last, aux):
    rows_here, dim = embeddings.shape
    k0 = factor_cols.shape[1]
    tile = rows_here // TILES
    rows = (last - first) * tile
    specs = [
        pl.BlockSpec(memory_space=pltpu.VMEM),
        pl.BlockSpec((tile, dim), lambda i: (i + first, 0)),
        pl.BlockSpec((tile, k0), lambda i: (i + first, 0)),
    ]
    args = (solved2, embeddings, factor_cols)
    if aux is not None:
        specs.append(pl.BlockSpec(memory_space=pl.ANY))
        args += (aux,)
    return pl.pallas_call(
        functools.partial(norms_kernel, first),
        grid=(last - first,),
        out_shape=jax.ShapeDtypeStruct((rows_here, 128), F32),
        in_specs=specs,
        out_specs=pl.BlockSpec((tile, 128), lambda i: (i + first, 0)),
        input_output_aliases={} if aux is None else {3: 0},
        compiler_params=pltpu.CompilerParams(
            dimension_semantics=("arbitrary",), vmem_limit_bytes=GRANT
        ),
        cost_estimate=pl.CostEstimate(
            flops=rows * (dim + k0) * 4, bytes_accessed=rows * (dim + k0) * 2, transcendentals=0
        ),
        name="row_norms",
    )(*args)


def ring(values, axis, pairs):
    return [lax.ppermute(v, axis, p) for v, p in zip(values, pairs)]


def body(embeddings, factor_cols, solved, pivots):
    rows_here, dim = embeddings.shape
    k0 = factor_cols.shape[1]
    total = pivots.shape[0]
    width = dim + k0 + 128
    tile = rows_here // TILES
    r = lax.axis_index("rows").astype(jnp.int32)
    c = lax.axis_index("cols").astype(jnp.int32)
    pos = jnp.stack([r * 16 + c, r // 2, r % 2])
    solved2 = solved.reshape(rows_here // 128, 128)
    piv2 = pivots.reshape(total // 128, 128)
    smem = pl.BlockSpec(memory_space=pltpu.SMEM)
    vmem = pl.BlockSpec(memory_space=pltpu.VMEM)
    hbm = pl.BlockSpec(memory_space=pltpu.HBM)
    small = pltpu.CompilerParams(vmem_limit_bytes=8 << 20)
    wide = lambda rows: jax.ShapeDtypeStruct((rows, width), BF16)
    swap = [(i, i ^ 1) for i in range(8)]
    zs = [[(i, i ^ (2 * k)) for i in range(8)] for k in range(1, RING)]
    xs = [[(i, i ^ (4 * k)) for i in range(16)] for k in range(1, RING)]
    ys = [[(i, i ^ k) for i in range(16)] for k in range(1, RING)]

    keep, send, loc = pl.pallas_call(
        own_kernel,
        out_shape=(wide(8), wide(8), jax.ShapeDtypeStruct((2 + PMAX,), jnp.int32)),
        in_specs=[smem, smem, vmem, smem, hbm, hbm],
        out_specs=(vmem, vmem, smem),
        scratch_shapes=[
            pltpu.VMEM((16 * PMAX, dim), BF16),
            pltpu.VMEM((16 * PMAX, k0), BF16),
            pltpu.SemaphoreType.DMA((2, PMAX)),
        ],
        compiler_params=pltpu.CompilerParams(vmem_limit_bytes=GRANT),
        name="own_rows",
    )(pos, pivots, piv2, solved2, embeddings, factor_cols)
    recv = lax.ppermute(send, "rows", swap)
    parts = pl.pallas_call(
        split_kernel, out_shape=(wide(8),) * RING, compiler_params=small, name="by_class",
    )(keep, recv)
    got = [parts[0]] + ring(parts[1:], "rows", zs)
    mine = pl.pallas_call(
        pack_kernel, out_shape=wide(16), compiler_params=small, name="pack",
    )(*got)
    counts, mine = lax.optimization_barrier((solved2, mine))
    got = [mine] + ring([mine] * 3, "cols", xs)
    aux = norms_part(counts, embeddings, factor_cols, 0, 3, None)
    aux, *got = lax.optimization_barrier((aux, *got))
    mine = pl.pallas_call(
        slots_kernel,
        out_shape=wide(total // CLASSES),
        in_specs=[smem] + [vmem] * RING,
        out_specs=vmem,
        compiler_params=small,
        name="slots",
    )(r.reshape(1), *got)
    counts, mine = lax.optimization_barrier((solved2, mine))
    got = [mine] + ring([mine] * 3, "cols", ys)
    aux = norms_part(counts, embeddings, factor_cols, 3, 6, aux)
    aux, *got = lax.optimization_barrier((aux, *got))
    mine = got[0] + got[1] + got[2] + got[3]
    counts, mine = lax.optimization_barrier((solved2, mine))
    got = [mine] + ring([mine] * 3, "rows", zs)
    aux = norms_part(counts, embeddings, factor_cols, 6, TILES, aux)
    aux, *got = lax.optimization_barrier((aux, *got))
    one = jnp.concatenate(got, axis=0)
    two = lax.ppermute(one, "rows", swap)

    new_cols, gains, best = main_call(loc, one, two, aux, embeddings, factor_cols)
    peers = lax.all_to_all(best.reshape(NDEV, 1, 128), AXES, 0, 0)
    return new_cols, gains.reshape(rows_here), jnp.max(peers)


def solution(mesh):
    in_specs = (P(AXES, None), P(AXES, None), P(AXES), P())
    out_specs = (P(AXES, None), P(AXES), P())
    return jax.shard_map(body, mesh=mesh, in_specs=in_specs, out_specs=out_specs, check_vma=False)
```

```python
import functools

import jax
import jax.numpy as jnp
from jax import lax
from jax.experimental import pallas as pl
from jax.experimental.pallas import tpu as pltpu
from jax.sharding import PartitionSpec as P

PMAX = 16
EPS = 1e-06
TAU = 6.0
RIDGE = 1.0
AXES = ("rows", "cols")
NDEV = 128
CLASSES = 8
RING = 4
SUB = 4
GRANT = 58 << 20
LOG2E = 1.4426950408889634
TILES = 8
BS = 32
F32 = jnp.float32
BF16 = jnp.bfloat16


def iota(shape, dim):
    return lax.broadcasted_iota(jnp.int32, shape, dim)


def learn(c):
    return (c * (16.0 - c) + 8.0) / 72.0


def own_kernel(
    pos_ref, piv_s, piv_v, solved_ref, emb_ref, fac_ref, keep_ref, send_ref, loc_ref, ebuf, fbuf, sem
):
    rows_here, dim = emb_ref.shape
    k0 = fac_ref.shape[1]
    total = piv_s.shape[0]
    first = pos_ref[0] * rows_here
    z = pos_ref[1]
    core = pos_ref[2]
    pv = piv_v[...]
    before = jnp.sum((pv < first).astype(F32)).astype(jnp.int32)
    upto = jnp.sum((pv < first + rows_here).astype(F32)).astype(jnp.int32)
    mine = upto - before
    loc_ref[0] = before
    loc_ref[1] = mine
    idx = []
    copies = []
    for s in range(PMAX):
        p = piv_s[jnp.minimum(before + s, total - 1)]
        i = jnp.clip(p - first, 0, rows_here - 1)
        loc_ref[2 + s] = i
        idx.append(i)
        base = pl.multiple_of((i // 16) * 16, 16)
        c1 = pltpu.make_async_copy(
            emb_ref.at[pl.ds(base, 16), :], ebuf.at[pl.ds(16 * s, 16), :], sem.at[0, s]
        )
        c2 = pltpu.make_async_copy(
            fac_ref.at[pl.ds(base, 16), :], fbuf.at[pl.ds(16 * s, 16), :], sem.at[1, s]
        )
        c1.start()
        c2.start()
        copies += [c1, c2]
    r = iota((16, 16 * PMAX), 0)
    q = iota((16, 16 * PMAX), 1)
    rc = iota((16, 128), 0)
    lane = iota((16, 128), 1)
    hot = jnp.zeros((16, 16 * PMAX), F32)
    tag = jnp.zeros((16, 128), F32)
    for s in range(PMAX):
        j = before + s
        cls = lax.rem(j, CLASSES)
        row = 2 * jnp.bitwise_xor(cls // 2, z) + s // CLASSES
        row = row + jnp.where(lax.rem(cls, 2) == core, 0, 8)
        row = jnp.where(s < mine, row, -1)
        hot = jnp.where((r == row) & (q == 16 * s + lax.rem(idx[s], 16)), 1.0, hot)
        c = solved_ref[idx[s] // 128, lax.rem(idx[s], 128)].astype(F32)
        tag = jnp.where(rc == row, jnp.where(lane == 0, c, (j + 1).astype(F32)), tag)
    hot = hot.astype(BF16)
    for c in copies:
        c.wait()
    e = jnp.dot(hot, ebuf[...], preferred_element_type=F32).astype(BF16)
    f = jnp.dot(hot, fbuf[...], preferred_element_type=F32).astype(BF16)
    t = tag.astype(BF16)
    for o, ref in ((0, keep_ref), (8, send_ref)):
        ref[:, 0:dim] = e[o : o + 8, :]
        ref[:, dim : dim + k0] = f[o : o + 8, :]
        ref[:, dim + k0 :] = t[o : o + 8, :]


def split_kernel(keep_ref, recv_ref, *outs):
    both = jnp.concatenate([keep_ref[...], recv_ref[...]], axis=0)
    r = iota((8, 16), 0)
    q = iota((8, 16), 1)
    for k, out in enumerate(outs):
        want = jnp.where(r < 2, 2 * k + r, 8 + 2 * k + r - 2)
        hot = ((q == want) & (r < 4)).astype(BF16)
        out[...] = jnp.dot(hot, both, preferred_element_type=F32).astype(BF16)


def pack_kernel(*refs):
    out = refs[-1]
    data = jnp.concatenate([ref[...] for ref in refs[:-1]], axis=0)
    r = iota((16, 32), 0)
    q = iota((16, 32), 1)
    hot = (q == 8 * (r // 4) + lax.rem(r, 4)).astype(BF16)
    out[...] = jnp.dot(hot, data, preferred_element_type=F32).astype(BF16)


def slots_kernel(cls_ref, *refs):
    out = refs[-1]
    slots, width = out.shape
    data = jnp.concatenate([ref[...] for ref in refs[:-1]], axis=0)
    ids = data[:, width - 127 : width - 126].astype(F32)
    want = (CLASSES * iota((data.shape[0], slots), 1) + cls_ref[0] + 1).astype(F32)
    hot = (ids == want).astype(BF16)
    out[...] = lax.dot_general(
        hot, data, (((0,), (0,)), ((), ())), preferred_element_type=F32
    ).astype(BF16)


def norms_kernel(first, solved_ref, emb_ref, fac_ref, *refs):
    aux_ref = refs[-1]
    i = pl.program_id(0) + first
    tile, dim = emb_ref.shape
    nchunk = tile // 128
    st = solved_ref[pl.ds(i * nchunk, nchunk), :].astype(F32)
    ey = iota((128, 128), 0) == iota((128, 128), 1)
    lane = iota((128, 128), 1)
    ndims = (((1,), (1,)), ((), ()))
    for c in range(nchunk):
        o = slice(128 * c, 128 * c + 128)
        x = emb_ref[o, :]
        f = fac_ref[o, :]
        xx = lax.dot_general(x, x, ndims, preferred_element_type=F32)
        ff = lax.dot_general(f, f, ndims, preferred_element_type=F32)
        ss = jnp.sum(jnp.where(ey, xx, 0.0), axis=1, keepdims=True)
        fs = jnp.sum(jnp.where(ey, ff, 0.0), axis=1, keepdims=True)
        a = 1.0 / jnp.sqrt(ss / dim + EPS)
        b = jnp.broadcast_to(st[c : c + 1, :], (128, 128))
        q = learn(jnp.sum(jnp.where(ey, b, 0.0), axis=1, keepdims=True))
        aux_ref[o, :] = jnp.where(lane == 0, a, jnp.where(lane == 1, q, q * q + RIDGE - fs))

def split3(x):
    h = x.astype(BF16)
    r = x - h.astype(F32)
    m = r.astype(BF16)
    l = (r - m.astype(F32)).astype(BF16)
    return h, m, l


def lanes(x, k):
    return jnp.broadcast_to(x[:, k : k + 1], x.shape)


def sublanes(x, k):
    return jnp.broadcast_to(x[k : k + 1, :], x.shape)


def eliminate(w):
    rows, width = w.shape
    groups = [
        [w[8 * g : 8 * g + 8, 128 * v : 128 * v + 128] for v in range(width // 128)]
        for g in range(rows // 8)
    ]
    srow = iota((8, 128), 0)
    done = []
    for t in range(rows // 8):
        cols = [lanes(groups[t][0], 8 * t + k) for k in range(8)]
        e = [[sublanes(cols[k], i) for k in range(i + 1)] for i in range(8)]
        below = {
            g: [lanes(groups[g][0], 8 * t + k) for k in range(8)]
            for g in range(t + 1, rows // 8)
        }
        tops = [[sublanes(x, j) for x in groups[t]] for j in range(8)]
        m = [[None] * 8 for _ in range(8)]
        n = [[None] * 8 for _ in range(8)]
        for k in range(8):
            inv = 1.0 / e[k][k]
            for i in range(k + 1, 8):
                m[i][k] = e[i][k] * inv
                for j in range(k + 1, i + 1):
                    e[i][j] = e[i][j] - m[i][k] * e[j][k]
            for j in range(k):
                acc = m[k][j]
                for l in range(j + 1, k):
                    acc = acc + m[k][l] * n[l][j]
                n[k][j] = -acc
        root = [1.0 / jnp.sqrt(e[k][k]) for k in range(8)]
        inv = [[root[i] * n[i][j] for j in range(i)] + [root[i]] for i in range(8)]
        cols = []
        for j in range(8):
            c = jnp.where(srow == j, inv[j][j], 0.0)
            for i in range(j + 1, 8):
                c = jnp.where(srow == i, inv[i][j], c)
            cols.append(c)
        out = []
        for v in range(width // 128):
            acc = cols[0] * tops[0][v]
            for j in range(1, 8):
                acc = acc + cols[j] * tops[j][v]
            out.append(acc)
        for g in range(t + 1, rows // 8):
            for j in range(8):
                c = below[g][0] * inv[j][0]
                for k in range(1, j + 1):
                    c = c + below[g][k] * inv[j][k]
                groups[g] = [x - c * sublanes(o, j) for x, o in zip(groups[g], out)]
        done.append(jnp.concatenate(out, axis=1))
    return jnp.concatenate(done, axis=0)


def main_kernel(
    loc_ref, one_ref, two_ref, aux_ref, emb_ref, fac_ref,
    out_ref, gains_ref, best_ref,
    piv, pvec, ar, minv, mt, panel, base,
):
    i = pl.program_id(0)
    tile, dim = emb_ref.shape
    k0 = fac_ref.shape[1]
    n = piv.shape[0]
    nchunk = tile // 128
    sub = tile // SUB
    tdims = (((0,), (0,)), ((), ()))
    ndims = (((1,), (1,)), ((), ()))

    @pl.when(i == 0)
    def _():
        jj = iota((n, n), 0)
        qq = iota((n, n), 1)
        eye = (jj == qq).astype(F32)
        data = jnp.concatenate([one_ref[...], two_ref[...]], axis=0)
        ids = data[:, dim + k0 + 1 : dim + k0 + 2].astype(F32)
        permt = (ids == (qq + 1).astype(F32)).astype(BF16)
        v = lax.dot_general(permt, data, tdims, preferred_element_type=F32)
        pb = v.astype(BF16)
        piv[...] = pb[:, 0 : dim + k0]
        cs = 1.0 / jnp.sqrt(
            jnp.sum(v[:, 0:dim] * v[:, 0:dim], axis=1, keepdims=True) / dim + EPS
        )
        cq = learn(v[:, dim + k0 : dim + k0 + 1])
        rs = jnp.sum(eye * cs, axis=0, keepdims=True) * (TAU * LOG2E / dim)
        rq = jnp.sum(eye * cq, axis=0, keepdims=True)
        pvec[0:1, :] = rs
        pvec[1:2, :] = rq
        dots = lax.dot_general(pb[:, 0:dim], piv[:, 0:dim], ndims, preferred_element_type=F32)
        shared = lax.dot_general(
            pb[:, dim : dim + k0], piv[:, dim : dim + k0], ndims, preferred_element_type=F32
        )
        similar = jnp.exp2(dots * (cs * rs) - TAU * LOG2E)
        ar[:, 0:n] = similar * (cq * rq) + RIDGE * eye - shared
        ar[:, n : 2 * n] = eye

    @pl.when(i < TILES)
    def _():
        for c in range(SUB):
            o = slice(sub * c, sub * c + sub)
            a = aux_ref[o, 0:1]
            q = aux_ref[o, 1:2]
            dots = lax.dot_general(
                emb_ref[o, :], piv[:, 0:dim], ndims, preferred_element_type=F32
            )
            shared = lax.dot_general(
                fac_ref[o, :], piv[:, dim : dim + k0], ndims, preferred_element_type=F32
            )
            similar = jnp.exp2(dots * (a * pvec[0:1, :]) - TAU * LOG2E)
            p = similar * (q * pvec[1:2, :]) - shared
            ph = p.astype(BF16)
            w = pl.ds(pl.multiple_of(i * tile + sub * c, 16), sub)
            panel[w, 0:n] = ph
            panel[w, n : 2 * n] = (p - ph.astype(F32)).astype(BF16)
            base[w, :] = jnp.broadcast_to(aux_ref[o, 2:3], (sub, 128))

        rows = pl.ds(pl.multiple_of(i * BS, BS), BS)
        shift = lax.rem(n - i * BS, n)
        a = pltpu.roll(ar[rows, 0:n], shift, 1)
        w = eliminate(jnp.concatenate([a, ar[rows, n : 2 * n]], axis=1))
        u = pltpu.roll(w[:, 0:n], i * BS, 1)
        m = w[:, n : 2 * n]
        minv[rows, :] = m
        uh, um, ul = split3(u)
        mh, mm, ml = split3(m)
        left = jnp.concatenate([uh, uh, um, uh, ul, um], axis=0)
        r_a = jnp.concatenate([uh, um, uh, ul, uh, um], axis=0)
        r_m = jnp.concatenate([mh, mm, mh, ml, mh, mm], axis=0)
        ar[:, 0:n] -= lax.dot_general(left, r_a, tdims, preferred_element_type=F32)
        ar[:, n : 2 * n] -= lax.dot_general(left, r_m, tdims, preferred_element_type=F32)

    @pl.when(i == TILES)
    def _():
        t = minv[...].T
        h = t.astype(BF16)
        mt[0:n, :] = h
        mt[n : 2 * n, :] = h
        mt[2 * n : 3 * n, :] = (t - h.astype(F32)).astype(BF16)
        best_ref[...] = jnp.full(best_ref.shape, -jnp.inf, F32)

        def ridge(s, carry):
            at = loc_ref[2 + s]
            w = pl.ds(pl.multiple_of((at // 16) * 16, 16), 16)
            p = panel[w, 0:n].astype(F32) + panel[w, n : 2 * n].astype(F32)
            here = (iota((16, n), 0) == lax.rem(at, 16)) & (iota((16, n), 1) == loc_ref[0] + s)
            p = p + jnp.where(here, RIDGE, 0.0)
            ph = p.astype(BF16)
            panel[w, 0:n] = ph
            panel[w, n : 2 * n] = (p - ph.astype(F32)).astype(BF16)
            return carry

        lax.fori_loop(0, jnp.minimum(loc_ref[1], PMAX), ridge, 0)

    @pl.when(i >= TILES)
    def _():
        t = i - TILES
        gs = []
        for c in range(SUB):
            o = slice(sub * c, sub * c + sub)
            w = pl.ds(pl.multiple_of(t * tile + sub * c, 16), sub)
            full = jnp.dot(panel[w, :], mt[0 : 2 * n, :], preferred_element_type=F32)
            full += jnp.dot(panel[w, 0:n], mt[2 * n : 3 * n, :], preferred_element_type=F32)
            out_ref[o, :] = full.astype(BF16)
            gs.append(base[w, :] - jnp.sum(full * full, axis=1, keepdims=True))
        g = jnp.concatenate(gs, axis=0)
        ey = iota((128, 128), 0) == iota((128, 128), 1)
        lines = []
        for c in range(nchunk):
            lines.append(
                jnp.sum(jnp.where(ey, g[128 * c : 128 * c + 128, :], 0.0), axis=0, keepdims=True)
            )
        lines = jnp.concatenate(lines, axis=0)
        gains_ref[pl.ds(t * nchunk, nchunk), :] = lines
        best_ref[...] = jnp.maximum(best_ref[...], jnp.max(lines))


def main_call(loc, one, two, aux, embeddings, factor_cols):
    rows_here, dim = embeddings.shape
    k0 = factor_cols.shape[1]
    total = one.shape[0] + two.shape[0]
    tile = rows_here // TILES
    smem = pl.BlockSpec(memory_space=pltpu.SMEM)
    vmem = pl.BlockSpec(memory_space=pltpu.VMEM)
    return pl.pallas_call(
        main_kernel,
        grid=(2 * TILES,),
        out_shape=(
            jax.ShapeDtypeStruct((rows_here, total), BF16),
            jax.ShapeDtypeStruct((rows_here // 128, 128), F32),
            jax.ShapeDtypeStruct((NDEV, 128), F32),
        ),
        in_specs=[
            smem, vmem, vmem,
            pl.BlockSpec((tile, 128), lambda i: (jnp.minimum(i, TILES - 1), 0)),
            pl.BlockSpec((tile, dim), lambda i: (jnp.minimum(i, TILES - 1), 0)),
            pl.BlockSpec((tile, k0), lambda i: (jnp.minimum(i, TILES - 1), 0)),
        ],
        out_specs=(
            pl.BlockSpec((tile, total), lambda i: (jnp.maximum(i - TILES, 0), 0)),
            pl.BlockSpec((rows_here // 128, 128), lambda i: (0, 0)),
            pl.BlockSpec((NDEV, 128), lambda i: (0, 0)),
        ),
        scratch_shapes=[
            pltpu.VMEM((total, dim + k0), BF16),
            pltpu.VMEM((8, total), F32),
            pltpu.VMEM((total, 2 * total), F32),
            pltpu.VMEM((total, total), F32),
            pltpu.VMEM((3 * total, total), BF16),
            pltpu.VMEM((rows_here, 2 * total), BF16),
            pltpu.VMEM((rows_here, 128), F32),
        ],
        compiler_params=pltpu.CompilerParams(
            dimension_semantics=("arbitrary",), vmem_limit_bytes=GRANT
        ),
        name="panel_factor",
    )(loc, one, two, aux, embeddings, factor_cols)


def norms_part(solved2, embeddings, factor_cols, first, last, aux):
    rows_here, dim = embeddings.shape
    k0 = factor_cols.shape[1]
    tile = rows_here // TILES
    rows = (last - first) * tile
    specs = [
        pl.BlockSpec(memory_space=pltpu.VMEM),
        pl.BlockSpec((tile, dim), lambda i: (i + first, 0)),
        pl.BlockSpec((tile, k0), lambda i: (i + first, 0)),
    ]
    args = (solved2, embeddings, factor_cols)
    if aux is not None:
        specs.append(pl.BlockSpec(memory_space=pl.ANY))
        args += (aux,)
    return pl.pallas_call(
        functools.partial(norms_kernel, first),
        grid=(last - first,),
        out_shape=jax.ShapeDtypeStruct((rows_here, 128), F32),
        in_specs=specs,
        out_specs=pl.BlockSpec((tile, 128), lambda i: (i + first, 0)),
        input_output_aliases={} if aux is None else {3: 0},
        compiler_params=pltpu.CompilerParams(
            dimension_semantics=("arbitrary",), vmem_limit_bytes=GRANT
        ),
        cost_estimate=pl.CostEstimate(
            flops=rows * (dim + k0) * 4, bytes_accessed=rows * (dim + k0) * 2, transcendentals=0
        ),
        name="row_norms",
    )(*args)


def ring(values, axis, pairs):
    return [lax.ppermute(v, axis, p) for v, p in zip(values, pairs)]


def body(embeddings, factor_cols, solved, pivots):
    rows_here, dim = embeddings.shape
    k0 = factor_cols.shape[1]
    total = pivots.shape[0]
    width = dim + k0 + 128
    tile = rows_here // TILES
    r = lax.axis_index("rows").astype(jnp.int32)
    c = lax.axis_index("cols").astype(jnp.int32)
    pos = jnp.stack([r * 16 + c, r // 2, r % 2])
    solved2 = solved.reshape(rows_here // 128, 128)
    piv2 = pivots.reshape(total // 128, 128)
    smem = pl.BlockSpec(memory_space=pltpu.SMEM)
    vmem = pl.BlockSpec(memory_space=pltpu.VMEM)
    hbm = pl.BlockSpec(memory_space=pltpu.HBM)
    small = pltpu.CompilerParams(vmem_limit_bytes=8 << 20)
    wide = lambda rows: jax.ShapeDtypeStruct((rows, width), BF16)
    swap = [(i, i ^ 1) for i in range(8)]
    zs = [[(i, i ^ (2 * k)) for i in range(8)] for k in range(1, RING)]
    xs = [[(i, i ^ (4 * k)) for i in range(16)] for k in range(1, RING)]
    ys = [[(i, i ^ k) for i in range(16)] for k in range(1, RING)]

    keep, send, loc = pl.pallas_call(
        own_kernel,
        out_shape=(wide(8), wide(8), jax.ShapeDtypeStruct((2 + PMAX,), jnp.int32)),
        in_specs=[smem, smem, vmem, smem, hbm, hbm],
        out_specs=(vmem, vmem, smem),
        scratch_shapes=[
            pltpu.VMEM((16 * PMAX, dim), BF16),
            pltpu.VMEM((16 * PMAX, k0), BF16),
            pltpu.SemaphoreType.DMA((2, PMAX)),
        ],
        compiler_params=pltpu.CompilerParams(vmem_limit_bytes=GRANT),
        name="own_rows",
    )(pos, pivots, piv2, solved2, embeddings, factor_cols)
    recv = lax.ppermute(send, "rows", swap)
    parts = pl.pallas_call(
        split_kernel, out_shape=(wide(8),) * RING, compiler_params=small, name="by_class",
    )(keep, recv)
    got = [parts[0]] + ring(parts[1:], "rows", zs)
    mine = pl.pallas_call(
        pack_kernel, out_shape=wide(16), compiler_params=small, name="pack",
    )(*got)
    counts, mine = lax.optimization_barrier((solved2, mine))
    got = [mine] + ring([mine] * 3, "cols", xs)
    aux = norms_part(counts, embeddings, factor_cols, 0, 3, None)
    aux, *got = lax.optimization_barrier((aux, *got))
    mine = pl.pallas_call(
        slots_kernel,
        out_shape=wide(total // CLASSES),
        in_specs=[smem] + [vmem] * RING,
        out_specs=vmem,
        compiler_params=small,
        name="slots",
    )(r.reshape(1), *got)
    counts, mine = lax.optimization_barrier((solved2, mine))
    got = [mine] + ring([mine] * 3, "cols", ys)
    aux = norms_part(counts, embeddings, factor_cols, 3, 6, aux)
    aux, *got = lax.optimization_barrier((aux, *got))
    mine = got[0] + got[1] + got[2] + got[3]
    counts, mine = lax.optimization_barrier((solved2, mine))
    got = [mine] + ring([mine] * 3, "rows", zs)
    aux = norms_part(counts, embeddings, factor_cols, 6, TILES, aux)
    aux, *got = lax.optimization_barrier((aux, *got))
    one = jnp.concatenate(got, axis=0)
    two = lax.ppermute(one, "rows", swap)

    new_cols, gains, best = main_call(loc, one, two, aux, embeddings, factor_cols)
    peers = lax.all_to_all(best.reshape(NDEV, 1, 128), AXES, 0, 0)
    return new_cols, gains.reshape(rows_here), jnp.max(peers)


def solution(mesh):
    in_specs = (P(AXES, None), P(AXES, None), P(AXES), P())
    out_specs = (P(AXES, None), P(AXES), P())
    return jax.shard_map(body, mesh=mesh, in_specs=in_specs, out_specs=out_specs, check_vma=False)
```

```python
import functools

import jax
import jax.numpy as jnp
from jax import lax
from jax.experimental import pallas as pl
from jax.experimental.pallas import tpu as pltpu
from jax.sharding import PartitionSpec as P

PMAX = 16
EPS = 1e-06
TAU = 6.0
RIDGE = 1.0
AXES = ("rows", "cols")
NDEV = 128
CLASSES = 8
RING = 4
SUB = 4
NORM_TILES = 14
SOLVE_SUB = 4
GRANT = 58 << 20
LOG2E = 1.4426950408889634
TILES = 8
BS = 32
F32 = jnp.float32
BF16 = jnp.bfloat16


def iota(shape, dim):
    return lax.broadcasted_iota(jnp.int32, shape, dim)


def learn(c):
    return (c * (16.0 - c) + 8.0) / 72.0


def own_kernel(
    dev_ref, piv_s, piv_v, solved_ref, emb_ref, fac_ref, send_ref, loc_ref, ebuf, fbuf, sem
):
    rows_here, dim = emb_ref.shape
    k0 = fac_ref.shape[1]
    total = piv_s.shape[0]
    first = dev_ref[0] * rows_here
    pv = piv_v[...]
    before = jnp.sum((pv < first).astype(F32)).astype(jnp.int32)
    upto = jnp.sum((pv < first + rows_here).astype(F32)).astype(jnp.int32)
    mine = upto - before
    loc_ref[0] = before
    loc_ref[1] = mine
    idx = []
    copies = []
    for s in range(PMAX):
        p = piv_s[jnp.minimum(before + s, total - 1)]
        i = jnp.clip(p - first, 0, rows_here - 1)
        loc_ref[2 + s] = i
        idx.append(i)
        base = pl.multiple_of((i // 16) * 16, 16)
        c1 = pltpu.make_async_copy(
            emb_ref.at[pl.ds(base, 16), :], ebuf.at[pl.ds(16 * s, 16), :], sem.at[0, s]
        )
        c2 = pltpu.make_async_copy(
            fac_ref.at[pl.ds(base, 16), :], fbuf.at[pl.ds(16 * s, 16), :], sem.at[1, s]
        )
        c1.start()
        c2.start()
        copies += [c1, c2]
    r = iota((16, 16 * PMAX), 0)
    q = iota((16, 16 * PMAX), 1)
    rc = iota((16, 128), 0)
    lane = iota((16, 128), 1)
    hot = jnp.zeros((16, 16 * PMAX), F32)
    tag = jnp.zeros((16, 128), F32)
    for s in range(PMAX):
        j = before + s
        row = jnp.where(s < mine, 2 * lax.rem(j, CLASSES) + s // CLASSES, -1)
        hot = jnp.where((r == row) & (q == 16 * s + lax.rem(idx[s], 16)), 1.0, hot)
        c = solved_ref[idx[s] // 128, lax.rem(idx[s], 128)].astype(F32)
        tag = jnp.where(rc == row, jnp.where(lane == 0, c, (j + 1).astype(F32)), tag)
    hot = hot.astype(BF16)
    for c in copies:
        c.wait()
    send_ref[:, 0:dim] = jnp.dot(hot, ebuf[...], preferred_element_type=F32).astype(BF16)
    send_ref[:, dim : dim + k0] = jnp.dot(hot, fbuf[...], preferred_element_type=F32).astype(BF16)
    send_ref[:, dim + k0 :] = tag.astype(BF16)


def slots_kernel(cls_ref, *refs):
    out = refs[-1]
    slots, width = out.shape
    data = jnp.concatenate([ref[...] for ref in refs[:-1]], axis=0)
    ids = data[:, width - 127 : width - 126].astype(F32)
    want = (CLASSES * iota((data.shape[0], slots), 1) + cls_ref[0] + 1).astype(F32)
    hot = (ids == want).astype(BF16)
    out[...] = lax.dot_general(
        hot, data, (((0,), (0,)), ((), ())), preferred_element_type=F32
    ).astype(BF16)


def norms_kernel(first, solved_ref, emb_ref, fac_ref, *refs):
    aux_ref = refs[-1]
    i = pl.program_id(0) + first
    tile, dim = emb_ref.shape
    nchunk = tile // 128
    st = solved_ref[pl.ds(i * nchunk, nchunk), :].astype(F32)
    ey = iota((128, 128), 0) == iota((128, 128), 1)
    lane = iota((128, 128), 1)
    ndims = (((1,), (1,)), ((), ()))
    for c in range(nchunk):
        o = slice(128 * c, 128 * c + 128)
        x = emb_ref[o, :].astype(F32)
        f = fac_ref[o, :]
        ff = lax.dot_general(f, f, ndims, preferred_element_type=F32)
        ss = jnp.sum(x * x, axis=1, keepdims=True)
        fs = jnp.sum(jnp.where(ey, ff, 0.0), axis=1, keepdims=True)
        a = 1.0 / jnp.sqrt(ss / dim + EPS)
        b = jnp.broadcast_to(st[c : c + 1, :], (128, 128))
        q = learn(jnp.sum(jnp.where(ey, b, 0.0), axis=1, keepdims=True))
        aux_ref[o, :] = jnp.where(lane == 0, q * q + RIDGE - fs, jnp.where(lane == 1, a, q))

def split3(x):
    h = x.astype(BF16)
    r = x - h.astype(F32)
    m = r.astype(BF16)
    l = (r - m.astype(F32)).astype(BF16)
    return h, m, l


def lanes(x, k):
    return jnp.broadcast_to(x[:, k : k + 1], x.shape)


def sublanes(x, k):
    return jnp.broadcast_to(x[k : k + 1, :], x.shape)


def eliminate(w):
    rows, width = w.shape
    groups = [
        [w[8 * g : 8 * g + 8, 128 * v : 128 * v + 128] for v in range(width // 128)]
        for g in range(rows // 8)
    ]
    srow = iota((8, 128), 0)
    done = []
    for t in range(rows // 8):
        cols = [lanes(groups[t][0], 8 * t + k) for k in range(8)]
        e = [[sublanes(cols[k], i) for k in range(i + 1)] for i in range(8)]
        below = {
            g: [lanes(groups[g][0], 8 * t + k) for k in range(8)]
            for g in range(t + 1, rows // 8)
        }
        tops = [[sublanes(x, j) for x in groups[t]] for j in range(8)]
        m = [[None] * 8 for _ in range(8)]
        n = [[None] * 8 for _ in range(8)]
        for k in range(8):
            inv = 1.0 / e[k][k]
            for i in range(k + 1, 8):
                m[i][k] = e[i][k] * inv
                for j in range(k + 1, i + 1):
                    e[i][j] = e[i][j] - m[i][k] * e[j][k]
            for j in range(k):
                acc = m[k][j]
                for l in range(j + 1, k):
                    acc = acc + m[k][l] * n[l][j]
                n[k][j] = -acc
        root = [1.0 / jnp.sqrt(e[k][k]) for k in range(8)]
        inv = [[root[i] * n[i][j] for j in range(i)] + [root[i]] for i in range(8)]
        cols = []
        for j in range(8):
            c = jnp.where(srow == j, inv[j][j], 0.0)
            for i in range(j + 1, 8):
                c = jnp.where(srow == i, inv[i][j], c)
            cols.append(c)
        out = []
        for v in range(width // 128):
            acc = cols[0] * tops[0][v]
            for j in range(1, 8):
                acc = acc + cols[j] * tops[j][v]
            out.append(acc)
        for g in range(t + 1, rows // 8):
            for j in range(8):
                c = below[g][0] * inv[j][0]
                for k in range(1, j + 1):
                    c = c + below[g][k] * inv[j][k]
                groups[g] = [x - c * sublanes(o, j) for x, o in zip(groups[g], out)]
        done.append(jnp.concatenate(out, axis=1))
    return jnp.concatenate(done, axis=0)


def main_kernel(
    loc_ref, one_ref, two_ref, aux_hbm, emb_hbm, fac_hbm,
    out_hbm, gains_ref, best_ref,
    piv, pvec, ar, minv, mt, panel, aux_ref, emb_ref, fac_ref, out_ref, sem, out_sem,
):
    rows_here, dim = emb_ref.shape
    tile = rows_here // TILES
    k0 = fac_ref.shape[1]
    n = piv.shape[0]

    def fetch(t):
        w = pl.ds(pl.multiple_of(t * tile, tile), tile)
        return [
            pltpu.make_async_copy(src.at[w, :], dst.at[w, :], sem.at[k, t])
            for k, (src, dst) in enumerate(
                ((aux_hbm, aux_ref), (emb_hbm, emb_ref), (fac_hbm, fac_ref))
            )
        ]

    for t in range(TILES):
        for c in fetch(t):
            c.start()

    nchunk = tile // 128
    sub = tile // SUB
    tdims = (((0,), (0,)), ((), ()))
    ndims = (((1,), (1,)), ((), ()))

    jj = iota((n, n), 0)
    qq = iota((n, n), 1)
    eye = (jj == qq).astype(F32)
    data = jnp.concatenate([one_ref[...], two_ref[...]], axis=0)
    ids = data[:, dim + k0 + 1 : dim + k0 + 2].astype(F32)
    permt = (ids == (qq + 1).astype(F32)).astype(BF16)
    v = lax.dot_general(permt, data, tdims, preferred_element_type=F32)
    pb = v.astype(BF16)
    piv[...] = pb[:, 0 : dim + k0]
    cs = 1.0 / jnp.sqrt(
        jnp.sum(v[:, 0:dim] * v[:, 0:dim], axis=1, keepdims=True) / dim + EPS
    )
    cq = learn(v[:, dim + k0 : dim + k0 + 1])
    rs = jnp.sum(eye * cs, axis=0, keepdims=True) * (TAU * LOG2E / dim)
    rq = jnp.sum(eye * cq, axis=0, keepdims=True)
    pvec[0:1, :] = rs
    pvec[1:2, :] = rq
    dots = lax.dot_general(pb[:, 0:dim], piv[:, 0:dim], ndims, preferred_element_type=F32)
    shared = lax.dot_general(
        pb[:, dim : dim + k0], piv[:, dim : dim + k0], ndims, preferred_element_type=F32
    )
    similar = jnp.exp2(dots * (cs * rs) - TAU * LOG2E)
    ar[:, 0:n] = similar * (cq * rq) + RIDGE * eye - shared
    ar[:, n : 2 * n] = eye

    def step(i, carry):
        for c in fetch(i):
            c.wait()
        for c in range(SUB):
            w = pl.ds(pl.multiple_of(i * tile + sub * c, 16), sub)
            a = aux_ref[w, 1:2]
            q = aux_ref[w, 2:3]
            dots = lax.dot_general(
                emb_ref[w, :], piv[:, 0:dim], ndims, preferred_element_type=F32
            )
            shared = lax.dot_general(
                fac_ref[w, :], piv[:, dim : dim + k0], ndims, preferred_element_type=F32
            )
            similar = jnp.exp2(dots * (a * pvec[0:1, :]) - TAU * LOG2E)
            p = similar * (q * pvec[1:2, :]) - shared
            ph = p.astype(BF16)
            panel[w, 0:n] = ph
            panel[w, n : 2 * n] = (p - ph.astype(F32)).astype(BF16)

        rows = pl.ds(pl.multiple_of(i * BS, BS), BS)
        shift = lax.rem(n - i * BS, n)
        a = pltpu.roll(ar[rows, 0:n], shift, 1)
        w = eliminate(jnp.concatenate([a, ar[rows, n : 2 * n]], axis=1))
        u = pltpu.roll(w[:, 0:n], i * BS, 1)
        m = w[:, n : 2 * n]
        minv[rows, :] = m
        uh, um, ul = split3(u)
        mh, mm, ml = split3(m)
        left = jnp.concatenate([uh, uh, um, uh, ul, um], axis=0)
        r_a = jnp.concatenate([uh, um, uh, ul, uh, um], axis=0)
        r_m = jnp.concatenate([mh, mm, mh, ml, mh, mm], axis=0)
        ar[:, 0:n] -= lax.dot_general(left, r_a, tdims, preferred_element_type=F32)
        ar[:, n : 2 * n] -= lax.dot_general(left, r_m, tdims, preferred_element_type=F32)
        return carry

    lax.fori_loop(0, TILES, step, 0)

    t = minv[...].T
    h = t.astype(BF16)
    mt[0:n, :] = h
    mt[n : 2 * n, :] = h
    mt[2 * n : 3 * n, :] = (t - h.astype(F32)).astype(BF16)
    best_ref[...] = jnp.full(best_ref.shape, -jnp.inf, F32)

    def ridge(s, carry):
        at = loc_ref[2 + s]
        w = pl.ds(pl.multiple_of((at // 16) * 16, 16), 16)
        p = panel[w, 0:n].astype(F32) + panel[w, n : 2 * n].astype(F32)
        here = (iota((16, n), 0) == lax.rem(at, 16)) & (iota((16, n), 1) == loc_ref[0] + s)
        p = p + jnp.where(here, RIDGE, 0.0)
        ph = p.astype(BF16)
        panel[w, 0:n] = ph
        panel[w, n : 2 * n] = (p - ph.astype(F32)).astype(BF16)
        return carry

    lax.fori_loop(0, jnp.minimum(loc_ref[1], PMAX), ridge, 0)

    def store(t):
        w = pl.ds(pl.multiple_of(t * tile, tile), tile)
        return pltpu.make_async_copy(out_ref.at[w, :], out_hbm.at[w, :], out_sem.at[t])

    def solve(t, carry):
        gs = []
        part = tile // SOLVE_SUB
        for c in range(SOLVE_SUB):
            w = pl.ds(pl.multiple_of(t * tile + part * c, 16), part)
            both = jnp.concatenate([panel[w, :], panel[w, 0:n]], axis=1)
            full = jnp.dot(both, mt[...], preferred_element_type=F32)
            out_ref[w, :] = full.astype(BF16)
            gs.append(aux_ref[w, 0:1] - jnp.sum(full * full, axis=1, keepdims=True))
        g = jnp.concatenate(gs, axis=0)
        ey = iota((128, 128), 0) == iota((128, 128), 1)
        lines = []
        for c in range(nchunk):
            b = jnp.broadcast_to(g[128 * c : 128 * c + 128, :], (128, 128))
            lines.append(jnp.sum(jnp.where(ey, b, 0.0), axis=0, keepdims=True))
        lines = jnp.concatenate(lines, axis=0)
        gains_ref[pl.ds(t * nchunk, nchunk), :] = lines
        best_ref[...] = jnp.maximum(best_ref[...], jnp.max(lines))
        store(t).start()
        return carry

    lax.fori_loop(0, TILES, solve, 0)
    for t in range(TILES):
        store(t).wait()


def main_call(loc, one, two, aux, embeddings, factor_cols):
    rows_here, dim = embeddings.shape
    k0 = factor_cols.shape[1]
    total = one.shape[0] + two.shape[0]
    tile = rows_here // TILES
    smem = pl.BlockSpec(memory_space=pltpu.SMEM)
    vmem = pl.BlockSpec(memory_space=pltpu.VMEM)
    hbm = pl.BlockSpec(memory_space=pltpu.HBM)
    return pl.pallas_call(
        main_kernel,
        out_shape=(
            jax.ShapeDtypeStruct((rows_here, total), BF16),
            jax.ShapeDtypeStruct((rows_here // 128, 128), F32),
            jax.ShapeDtypeStruct((NDEV, 128), F32),
        ),
        in_specs=[smem, vmem, vmem, hbm, hbm, hbm],
        out_specs=(hbm, vmem, vmem),
        scratch_shapes=[
            pltpu.VMEM((total, dim + k0), BF16),
            pltpu.VMEM((8, total), F32),
            pltpu.VMEM((total, 2 * total), F32),
            pltpu.VMEM((total, total), F32),
            pltpu.VMEM((3 * total, total), BF16),
            pltpu.VMEM((rows_here, 2 * total), BF16),
            pltpu.VMEM((rows_here, 128), F32),
            pltpu.VMEM((rows_here, dim), BF16),
            pltpu.VMEM((rows_here, k0), BF16),
            pltpu.VMEM((rows_here, total), BF16),
            pltpu.SemaphoreType.DMA((3, TILES)),
            pltpu.SemaphoreType.DMA((TILES,)),
        ],
        compiler_params=pltpu.CompilerParams(vmem_limit_bytes=GRANT),
        name="panel_factor",
    )(loc, one, two, aux, embeddings, factor_cols)


def norms_part(solved2, embeddings, factor_cols, first, last, aux):
    rows_here, dim = embeddings.shape
    k0 = factor_cols.shape[1]
    tile = rows_here // NORM_TILES
    rows = (last - first) * tile
    specs = [
        pl.BlockSpec(memory_space=pltpu.VMEM),
        pl.BlockSpec((tile, dim), lambda i: (i + first, 0)),
        pl.BlockSpec((tile, k0), lambda i: (i + first, 0)),
    ]
    args = (solved2, embeddings, factor_cols)
    if aux is not None:
        specs.append(pl.BlockSpec(memory_space=pl.ANY))
        args += (aux,)
    return pl.pallas_call(
        functools.partial(norms_kernel, first),
        grid=(last - first,),
        out_shape=jax.ShapeDtypeStruct((rows_here, 128), F32),
        in_specs=specs,
        out_specs=pl.BlockSpec((tile, 128), lambda i: (i + first, 0)),
        input_output_aliases={} if aux is None else {3: 0},
        compiler_params=pltpu.CompilerParams(
            dimension_semantics=("arbitrary",), vmem_limit_bytes=GRANT
        ),
        cost_estimate=pl.CostEstimate(
            flops=rows * (dim + k0) * 4, bytes_accessed=rows * (dim + k0) * 2, transcendentals=0
        ),
        name="row_norms",
    )(*args)


def ring(values, axis, pairs):
    return [lax.ppermute(v, axis, p) for v, p in zip(values, pairs)]


def body(embeddings, factor_cols, solved, pivots):
    rows_here, dim = embeddings.shape
    k0 = factor_cols.shape[1]
    total = pivots.shape[0]
    width = dim + k0 + 128
    tile = rows_here // TILES
    r = lax.axis_index("rows").astype(jnp.int32)
    c = lax.axis_index("cols").astype(jnp.int32)
    dev = (r * 16 + c).reshape(1)
    solved2 = solved.reshape(rows_here // 128, 128)
    piv2 = pivots.reshape(total // 128, 128)
    smem = pl.BlockSpec(memory_space=pltpu.SMEM)
    vmem = pl.BlockSpec(memory_space=pltpu.VMEM)
    hbm = pl.BlockSpec(memory_space=pltpu.HBM)
    small = pltpu.CompilerParams(vmem_limit_bytes=8 << 20)
    wide = lambda rows: jax.ShapeDtypeStruct((rows, width), BF16)
    swap = [(i, i ^ 1) for i in range(8)]
    zs = [[(i, i ^ (2 * k)) for i in range(8)] for k in range(1, RING)]
    xs = [[(i, i ^ (4 * k)) for i in range(16)] for k in range(1, RING)]
    ys = [[(i, i ^ k) for i in range(16)] for k in range(1, RING)]

    send, loc = pl.pallas_call(
        own_kernel,
        out_shape=(wide(16), jax.ShapeDtypeStruct((2 + PMAX,), jnp.int32)),
        in_specs=[smem, smem, vmem, smem, hbm, hbm],
        out_specs=(vmem, smem),
        scratch_shapes=[
            pltpu.VMEM((16 * PMAX, dim), BF16),
            pltpu.VMEM((16 * PMAX, k0), BF16),
            pltpu.SemaphoreType.DMA((2, PMAX)),
        ],
        compiler_params=pltpu.CompilerParams(vmem_limit_bytes=GRANT),
        name="own_rows",
    )(dev, pivots, piv2, solved2, embeddings, factor_cols)
    mine = lax.all_to_all(send.reshape(CLASSES, 2, width), "rows", 0, 0).reshape(16, width)
    counts, mine = lax.optimization_barrier((solved2, mine))
    got = [mine] + ring([mine] * 3, "cols", xs)
    aux = norms_part(counts, embeddings, factor_cols, 0, 5, None)
    aux, *got = lax.optimization_barrier((aux, *got))
    mine = pl.pallas_call(
        slots_kernel,
        out_shape=wide(total // CLASSES),
        in_specs=[smem] + [vmem] * RING,
        out_specs=vmem,
        compiler_params=small,
        name="slots",
    )(r.reshape(1), *got)
    counts, mine = lax.optimization_barrier((solved2, mine))
    got = [mine] + ring([mine] * 3, "cols", ys)
    aux = norms_part(counts, embeddings, factor_cols, 5, 10, aux)
    aux, *got = lax.optimization_barrier((aux, *got))
    mine = got[0] + got[1] + got[2] + got[3]
    counts, mine = lax.optimization_barrier((solved2, mine))
    got = [mine] + ring([mine] * 3, "rows", zs)
    aux = norms_part(counts, embeddings, factor_cols, 10, NORM_TILES, aux)
    aux, *got = lax.optimization_barrier((aux, *got))
    one = jnp.concatenate(got, axis=0)
    two = lax.ppermute(one, "rows", swap)

    new_cols, gains, best = main_call(loc, one, two, aux, embeddings, factor_cols)
    peers = lax.all_to_all(best.reshape(NDEV, 1, 128), AXES, 0, 0)
    return new_cols, gains.reshape(rows_here), jnp.max(peers)


def solution(mesh):
    in_specs = (P(AXES, None), P(AXES, None), P(AXES), P())
    out_specs = (P(AXES, None), P(AXES), P())
    return jax.shard_map(body, mesh=mesh, in_specs=in_specs, out_specs=out_specs, check_vma=False)
```

```python
import functools

import jax
import jax.numpy as jnp
from jax import lax
from jax.experimental import pallas as pl
from jax.experimental.pallas import tpu as pltpu
from jax.sharding import PartitionSpec as P

PMAX = 16
EPS = 1e-06
TAU = 6.0
RIDGE = 1.0
AXES = ("rows", "cols")
NDEV = 128
CLASSES = 8
RING = 4
SUB = 4
NORM_TILES = 14
SOLVE_SUB = 4
GRANT = 58 << 20
LOG2E = 1.4426950408889634
TILES = 8
BS = 32
F32 = jnp.float32
BF16 = jnp.bfloat16


def iota(shape, dim):
    return lax.broadcasted_iota(jnp.int32, shape, dim)


def learn(c):
    return (c * (16.0 - c) + 8.0) / 72.0


def own_kernel(
    dev_ref, piv_s, piv_v, solved_ref, emb_ref, fac_ref, send_ref, loc_ref, ebuf, fbuf, sem
):
    rows_here, dim = emb_ref.shape
    k0 = fac_ref.shape[1]
    total = piv_s.shape[0]
    first = dev_ref[0] * rows_here
    pv = piv_v[...]
    before = jnp.sum((pv < first).astype(F32)).astype(jnp.int32)
    upto = jnp.sum((pv < first + rows_here).astype(F32)).astype(jnp.int32)
    mine = upto - before
    loc_ref[0] = before
    loc_ref[1] = mine
    idx = []
    copies = []
    for s in range(PMAX):
        p = piv_s[jnp.minimum(before + s, total - 1)]
        i = jnp.clip(p - first, 0, rows_here - 1)
        loc_ref[2 + s] = i
        idx.append(i)
        base = pl.multiple_of((i // 16) * 16, 16)
        c1 = pltpu.make_async_copy(
            emb_ref.at[pl.ds(base, 16), :], ebuf.at[pl.ds(16 * s, 16), :], sem.at[0, s]
        )
        c2 = pltpu.make_async_copy(
            fac_ref.at[pl.ds(base, 16), :], fbuf.at[pl.ds(16 * s, 16), :], sem.at[1, s]
        )
        c1.start()
        c2.start()
        copies += [c1, c2]
    r = iota((16, 16 * PMAX), 0)
    q = iota((16, 16 * PMAX), 1)
    rc = iota((16, 128), 0)
    lane = iota((16, 128), 1)
    hot = jnp.zeros((16, 16 * PMAX), F32)
    tag = jnp.zeros((16, 128), F32)
    for s in range(PMAX):
        j = before + s
        row = jnp.where(s < mine, 2 * lax.rem(j, CLASSES) + s // CLASSES, -1)
        hot = jnp.where((r == row) & (q == 16 * s + lax.rem(idx[s], 16)), 1.0, hot)
        c = solved_ref[idx[s] // 128, lax.rem(idx[s], 128)].astype(F32)
        tag = jnp.where(rc == row, jnp.where(lane == 0, c, (j + 1).astype(F32)), tag)
    hot = hot.astype(BF16)
    for c in copies:
        c.wait()
    send_ref[:, 0:dim] = jnp.dot(hot, ebuf[...], preferred_element_type=F32).astype(BF16)
    send_ref[:, dim : dim + k0] = jnp.dot(hot, fbuf[...], preferred_element_type=F32).astype(BF16)
    send_ref[:, dim + k0 :] = tag.astype(BF16)


def slots_kernel(cls_ref, *refs):
    out = refs[-1]
    slots, width = out.shape
    data = jnp.concatenate([ref[...] for ref in refs[:-1]], axis=0)
    ids = data[:, width - 127 : width - 126].astype(F32)
    want = (CLASSES * iota((data.shape[0], slots), 1) + cls_ref[0] + 1).astype(F32)
    hot = (ids == want).astype(BF16)
    out[...] = lax.dot_general(
        hot, data, (((0,), (0,)), ((), ())), preferred_element_type=F32
    ).astype(BF16)


def norms_kernel(first, solved_ref, emb_hbm, fac_hbm, *refs):
    aux_hbm, emb_ref, fac_ref, aux_ref, sem, out_sem = refs[-6:]
    rows, dim = emb_ref.shape
    tile = emb_hbm.shape[0] // NORM_TILES
    nchunk = tile // 128
    ey = iota((128, 128), 0) == iota((128, 128), 1)
    lane = iota((128, 128), 1)
    ndims = (((1,), (1,)), ((), ()))

    def fetch(t):
        src = pl.ds(pl.multiple_of((first + t) * tile, tile), tile)
        dst = pl.ds(pl.multiple_of(t * tile, tile), tile)
        return [
            pltpu.make_async_copy(x.at[src, :], y.at[dst, :], sem.at[k, t])
            for k, (x, y) in enumerate(((emb_hbm, emb_ref), (fac_hbm, fac_ref)))
        ]

    def store(t):
        src = pl.ds(pl.multiple_of(t * tile, tile), tile)
        dst = pl.ds(pl.multiple_of((first + t) * tile, tile), tile)
        return pltpu.make_async_copy(aux_ref.at[src, :], aux_hbm.at[dst, :], out_sem.at[t])

    for t in range(rows // tile):
        for c in fetch(t):
            c.start()

    def step(t, carry):
        st = solved_ref[pl.ds((first + t) * nchunk, nchunk), :].astype(F32)
        for c in fetch(t):
            c.wait()
        for c in range(nchunk):
            o = pl.ds(pl.multiple_of(t * tile + 128 * c, 128), 128)
            x = emb_ref[o, :].astype(F32)
            f = fac_ref[o, :]
            ff = lax.dot_general(f, f, ndims, preferred_element_type=F32)
            ss = jnp.sum(x * x, axis=1, keepdims=True)
            fs = jnp.sum(jnp.where(ey, ff, 0.0), axis=1, keepdims=True)
            a = 1.0 / jnp.sqrt(ss / dim + EPS)
            b = jnp.broadcast_to(st[c : c + 1, :], (128, 128))
            q = learn(jnp.sum(jnp.where(ey, b, 0.0), axis=1, keepdims=True))
            aux_ref[o, :] = jnp.where(
                lane == 0, q * q + RIDGE - fs, jnp.where(lane == 1, a, q)
            )
        store(t).start()
        return carry

    lax.fori_loop(0, rows // tile, step, 0)
    for t in range(rows // tile):
        store(t).wait()


def split3(x):
    h = x.astype(BF16)
    r = x - h.astype(F32)
    m = r.astype(BF16)
    l = (r - m.astype(F32)).astype(BF16)
    return h, m, l


def lanes(x, k):
    return jnp.broadcast_to(x[:, k : k + 1], x.shape)


def sublanes(x, k):
    return jnp.broadcast_to(x[k : k + 1, :], x.shape)


def eliminate(w):
    rows, width = w.shape
    groups = [
        [w[8 * g : 8 * g + 8, 128 * v : 128 * v + 128] for v in range(width // 128)]
        for g in range(rows // 8)
    ]
    srow = iota((8, 128), 0)
    done = []
    for t in range(rows // 8):
        cols = [lanes(groups[t][0], 8 * t + k) for k in range(8)]
        e = [[sublanes(cols[k], i) for k in range(i + 1)] for i in range(8)]
        below = {
            g: [lanes(groups[g][0], 8 * t + k) for k in range(8)]
            for g in range(t + 1, rows // 8)
        }
        tops = [[sublanes(x, j) for x in groups[t]] for j in range(8)]
        m = [[None] * 8 for _ in range(8)]
        n = [[None] * 8 for _ in range(8)]
        for k in range(8):
            inv = 1.0 / e[k][k]
            for i in range(k + 1, 8):
                m[i][k] = e[i][k] * inv
                for j in range(k + 1, i + 1):
                    e[i][j] = e[i][j] - m[i][k] * e[j][k]
            for j in range(k):
                acc = m[k][j]
                for l in range(j + 1, k):
                    acc = acc + m[k][l] * n[l][j]
                n[k][j] = -acc
        root = [1.0 / jnp.sqrt(e[k][k]) for k in range(8)]
        inv = [[root[i] * n[i][j] for j in range(i)] + [root[i]] for i in range(8)]
        cols = []
        for j in range(8):
            c = jnp.where(srow == j, inv[j][j], 0.0)
            for i in range(j + 1, 8):
                c = jnp.where(srow == i, inv[i][j], c)
            cols.append(c)
        out = []
        for v in range(width // 128):
            acc = cols[0] * tops[0][v]
            for j in range(1, 8):
                acc = acc + cols[j] * tops[j][v]
            out.append(acc)
        for g in range(t + 1, rows // 8):
            for j in range(8):
                c = below[g][0] * inv[j][0]
                for k in range(1, j + 1):
                    c = c + below[g][k] * inv[j][k]
                groups[g] = [x - c * sublanes(o, j) for x, o in zip(groups[g], out)]
        done.append(jnp.concatenate(out, axis=1))
    return jnp.concatenate(done, axis=0)


def main_kernel(
    loc_ref, one_ref, two_ref, aux_hbm, emb_hbm, fac_hbm,
    out_hbm, gains_ref, best_ref,
    piv, pvec, ar, minv, mt, panel, aux_ref, emb_ref, fac_ref, out_ref, sem, out_sem,
):
    rows_here, dim = emb_ref.shape
    tile = rows_here // TILES
    k0 = fac_ref.shape[1]
    n = piv.shape[0]

    def fetch(t):
        w = pl.ds(pl.multiple_of(t * tile, tile), tile)
        return [
            pltpu.make_async_copy(src.at[w, :], dst.at[w, :], sem.at[k, t])
            for k, (src, dst) in enumerate(
                ((aux_hbm, aux_ref), (emb_hbm, emb_ref), (fac_hbm, fac_ref))
            )
        ]

    for t in range(TILES):
        for c in fetch(t):
            c.start()

    nchunk = tile // 128
    sub = tile // SUB
    tdims = (((0,), (0,)), ((), ()))
    ndims = (((1,), (1,)), ((), ()))

    jj = iota((n, n), 0)
    qq = iota((n, n), 1)
    eye = (jj == qq).astype(F32)
    data = jnp.concatenate([one_ref[...], two_ref[...]], axis=0)
    ids = data[:, dim + k0 + 1 : dim + k0 + 2].astype(F32)
    permt = (ids == (qq + 1).astype(F32)).astype(BF16)
    v = lax.dot_general(permt, data, tdims, preferred_element_type=F32)
    pb = v.astype(BF16)
    piv[...] = pb[:, 0 : dim + k0]
    cs = 1.0 / jnp.sqrt(
        jnp.sum(v[:, 0:dim] * v[:, 0:dim], axis=1, keepdims=True) / dim + EPS
    )
    cq = learn(v[:, dim + k0 : dim + k0 + 1])
    rs = jnp.sum(eye * cs, axis=0, keepdims=True) * (TAU * LOG2E / dim)
    rq = jnp.sum(eye * cq, axis=0, keepdims=True)
    pvec[0:1, :] = rs
    pvec[1:2, :] = rq
    dots = lax.dot_general(pb[:, 0:dim], piv[:, 0:dim], ndims, preferred_element_type=F32)
    shared = lax.dot_general(
        pb[:, dim : dim + k0], piv[:, dim : dim + k0], ndims, preferred_element_type=F32
    )
    similar = jnp.exp2(dots * (cs * rs) - TAU * LOG2E)
    ar[:, 0:n] = similar * (cq * rq) + RIDGE * eye - shared
    ar[:, n : 2 * n] = eye

    def step(i, carry):
        for c in fetch(i):
            c.wait()
        for c in range(SUB):
            w = pl.ds(pl.multiple_of(i * tile + sub * c, 16), sub)
            a = aux_ref[w, 1:2]
            q = aux_ref[w, 2:3]
            dots = lax.dot_general(
                emb_ref[w, :], piv[:, 0:dim], ndims, preferred_element_type=F32
            )
            shared = lax.dot_general(
                fac_ref[w, :], piv[:, dim : dim + k0], ndims, preferred_element_type=F32
            )
            similar = jnp.exp2(dots * (a * pvec[0:1, :]) - TAU * LOG2E)
            p = similar * (q * pvec[1:2, :]) - shared
            ph = p.astype(BF16)
            panel[w, 0:n] = ph
            panel[w, n : 2 * n] = (p - ph.astype(F32)).astype(BF16)

        rows = pl.ds(pl.multiple_of(i * BS, BS), BS)
        shift = lax.rem(n - i * BS, n)
        a = pltpu.roll(ar[rows, 0:n], shift, 1)
        w = eliminate(jnp.concatenate([a, ar[rows, n : 2 * n]], axis=1))
        u = pltpu.roll(w[:, 0:n], i * BS, 1)
        m = w[:, n : 2 * n]
        minv[rows, :] = m
        uh, um, ul = split3(u)
        mh, mm, ml = split3(m)
        left = jnp.concatenate([uh, uh, um, uh, ul, um], axis=0)
        r_a = jnp.concatenate([uh, um, uh, ul, uh, um], axis=0)
        r_m = jnp.concatenate([mh, mm, mh, ml, mh, mm], axis=0)
        ar[:, 0:n] -= lax.dot_general(left, r_a, tdims, preferred_element_type=F32)
        ar[:, n : 2 * n] -= lax.dot_general(left, r_m, tdims, preferred_element_type=F32)
        return carry

    lax.fori_loop(0, TILES, step, 0)

    t = minv[...].T
    h = t.astype(BF16)
    mt[0:n, :] = h
    mt[n : 2 * n, :] = h
    mt[2 * n : 3 * n, :] = (t - h.astype(F32)).astype(BF16)
    best_ref[...] = jnp.full(best_ref.shape, -jnp.inf, F32)

    def ridge(s, carry):
        at = loc_ref[2 + s]
        w = pl.ds(pl.multiple_of((at // 16) * 16, 16), 16)
        p = panel[w, 0:n].astype(F32) + panel[w, n : 2 * n].astype(F32)
        here = (iota((16, n), 0) == lax.rem(at, 16)) & (iota((16, n), 1) == loc_ref[0] + s)
        p = p + jnp.where(here, RIDGE, 0.0)
        ph = p.astype(BF16)
        panel[w, 0:n] = ph
        panel[w, n : 2 * n] = (p - ph.astype(F32)).astype(BF16)
        return carry

    lax.fori_loop(0, jnp.minimum(loc_ref[1], PMAX), ridge, 0)

    def store(t):
        w = pl.ds(pl.multiple_of(t * tile, tile), tile)
        return pltpu.make_async_copy(out_ref.at[w, :], out_hbm.at[w, :], out_sem.at[t])

    def solve(t, carry):
        gs = []
        part = tile // SOLVE_SUB
        for c in range(SOLVE_SUB):
            w = pl.ds(pl.multiple_of(t * tile + part * c, 16), part)
            both = jnp.concatenate([panel[w, :], panel[w, 0:n]], axis=1)
            full = jnp.dot(both, mt[...], preferred_element_type=F32)
            out_ref[w, :] = full.astype(BF16)
            gs.append(aux_ref[w, 0:1] - jnp.sum(full * full, axis=1, keepdims=True))
        g = jnp.concatenate(gs, axis=0)
        ey = iota((128, 128), 0) == iota((128, 128), 1)
        lines = []
        for c in range(nchunk):
            b = jnp.broadcast_to(g[128 * c : 128 * c + 128, :], (128, 128))
            lines.append(jnp.sum(jnp.where(ey, b, 0.0), axis=0, keepdims=True))
        lines = jnp.concatenate(lines, axis=0)
        gains_ref[pl.ds(t * nchunk, nchunk), :] = lines
        best_ref[...] = jnp.maximum(best_ref[...], jnp.max(lines))
        store(t).start()
        return carry

    lax.fori_loop(0, TILES, solve, 0)
    for t in range(TILES):
        store(t).wait()


def main_call(loc, one, two, aux, embeddings, factor_cols):
    rows_here, dim = embeddings.shape
    k0 = factor_cols.shape[1]
    total = one.shape[0] + two.shape[0]
    tile = rows_here // TILES
    smem = pl.BlockSpec(memory_space=pltpu.SMEM)
    vmem = pl.BlockSpec(memory_space=pltpu.VMEM)
    hbm = pl.BlockSpec(memory_space=pltpu.HBM)
    return pl.pallas_call(
        main_kernel,
        out_shape=(
            jax.ShapeDtypeStruct((rows_here, total), BF16),
            jax.ShapeDtypeStruct((rows_here // 128, 128), F32),
            jax.ShapeDtypeStruct((NDEV, 128), F32),
        ),
        in_specs=[smem, vmem, vmem, hbm, hbm, hbm],
        out_specs=(hbm, vmem, vmem),
        scratch_shapes=[
            pltpu.VMEM((total, dim + k0), BF16),
            pltpu.VMEM((8, total), F32),
            pltpu.VMEM((total, 2 * total), F32),
            pltpu.VMEM((total, total), F32),
            pltpu.VMEM((3 * total, total), BF16),
            pltpu.VMEM((rows_here, 2 * total), BF16),
            pltpu.VMEM((rows_here, 128), F32),
            pltpu.VMEM((rows_here, dim), BF16),
            pltpu.VMEM((rows_here, k0), BF16),
            pltpu.VMEM((rows_here, total), BF16),
            pltpu.SemaphoreType.DMA((3, TILES)),
            pltpu.SemaphoreType.DMA((TILES,)),
        ],
        compiler_params=pltpu.CompilerParams(vmem_limit_bytes=GRANT),
        name="panel_factor",
    )(loc, one, two, aux, embeddings, factor_cols)


def norms_part(solved2, embeddings, factor_cols, first, last, aux):
    rows_here, dim = embeddings.shape
    k0 = factor_cols.shape[1]
    tile = rows_here // NORM_TILES
    rows = (last - first) * tile
    hbm = pl.BlockSpec(memory_space=pltpu.HBM)
    specs = [pl.BlockSpec(memory_space=pltpu.VMEM), hbm, hbm]
    args = (solved2, embeddings, factor_cols)
    if aux is not None:
        specs.append(hbm)
        args += (aux,)
    return pl.pallas_call(
        functools.partial(norms_kernel, first),
        out_shape=jax.ShapeDtypeStruct((rows_here, 128), F32),
        in_specs=specs,
        out_specs=hbm,
        scratch_shapes=[
            pltpu.VMEM((rows, dim), BF16),
            pltpu.VMEM((rows, k0), BF16),
            pltpu.VMEM((rows, 128), F32),
            pltpu.SemaphoreType.DMA((2, last - first)),
            pltpu.SemaphoreType.DMA((last - first,)),
        ],
        input_output_aliases={} if aux is None else {3: 0},
        compiler_params=pltpu.CompilerParams(vmem_limit_bytes=GRANT),
        cost_estimate=pl.CostEstimate(
            flops=rows * (dim + k0) * 4, bytes_accessed=rows * (dim + k0) * 2, transcendentals=0
        ),
        name="row_norms",
    )(*args)


def ring(values, axis, pairs):
    return [lax.ppermute(v, axis, p) for v, p in zip(values, pairs)]


def body(embeddings, factor_cols, solved, pivots):
    rows_here, dim = embeddings.shape
    k0 = factor_cols.shape[1]
    total = pivots.shape[0]
    width = dim + k0 + 128
    tile = rows_here // TILES
    r = lax.axis_index("rows").astype(jnp.int32)
    c = lax.axis_index("cols").astype(jnp.int32)
    dev = (r * 16 + c).reshape(1)
    solved2 = solved.reshape(rows_here // 128, 128)
    piv2 = pivots.reshape(total // 128, 128)
    smem = pl.BlockSpec(memory_space=pltpu.SMEM)
    vmem = pl.BlockSpec(memory_space=pltpu.VMEM)
    hbm = pl.BlockSpec(memory_space=pltpu.HBM)
    small = pltpu.CompilerParams(vmem_limit_bytes=8 << 20)
    wide = lambda rows: jax.ShapeDtypeStruct((rows, width), BF16)
    swap = [(i, i ^ 1) for i in range(8)]
    zs = [[(i, i ^ (2 * k)) for i in range(8)] for k in range(1, RING)]
    xs = [[(i, i ^ (4 * k)) for i in range(16)] for k in range(1, RING)]
    ys = [[(i, i ^ k) for i in range(16)] for k in range(1, RING)]

    send, loc = pl.pallas_call(
        own_kernel,
        out_shape=(wide(16), jax.ShapeDtypeStruct((2 + PMAX,), jnp.int32)),
        in_specs=[smem, smem, vmem, smem, hbm, hbm],
        out_specs=(vmem, smem),
        scratch_shapes=[
            pltpu.VMEM((16 * PMAX, dim), BF16),
            pltpu.VMEM((16 * PMAX, k0), BF16),
            pltpu.SemaphoreType.DMA((2, PMAX)),
        ],
        compiler_params=pltpu.CompilerParams(vmem_limit_bytes=GRANT),
        name="own_rows",
    )(dev, pivots, piv2, solved2, embeddings, factor_cols)
    mine = lax.all_to_all(send.reshape(CLASSES, 2, width), "rows", 0, 0).reshape(16, width)
    counts, mine = lax.optimization_barrier((solved2, mine))
    got = [mine] + ring([mine] * 3, "cols", xs)
    aux = norms_part(counts, embeddings, factor_cols, 0, 5, None)
    aux, *got = lax.optimization_barrier((aux, *got))
    mine = pl.pallas_call(
        slots_kernel,
        out_shape=wide(total // CLASSES),
        in_specs=[smem] + [vmem] * RING,
        out_specs=vmem,
        compiler_params=small,
        name="slots",
    )(r.reshape(1), *got)
    counts, mine = lax.optimization_barrier((solved2, mine))
    got = [mine] + ring([mine] * 3, "cols", ys)
    aux = norms_part(counts, embeddings, factor_cols, 5, 10, aux)
    aux, *got = lax.optimization_barrier((aux, *got))
    mine = got[0] + got[1] + got[2] + got[3]
    counts, mine = lax.optimization_barrier((solved2, mine))
    got = [mine] + ring([mine] * 3, "rows", zs)
    aux = norms_part(counts, embeddings, factor_cols, 10, NORM_TILES, aux)
    aux, *got = lax.optimization_barrier((aux, *got))
    one = jnp.concatenate(got, axis=0)
    two = lax.ppermute(one, "rows", swap)

    new_cols, gains, best = main_call(loc, one, two, aux, embeddings, factor_cols)
    peers = lax.all_to_all(best.reshape(NDEV, 1, 128), AXES, 0, 0)
    return new_cols, gains.reshape(rows_here), jnp.max(peers)


def solution(mesh):
    in_specs = (P(AXES, None), P(AXES, None), P(AXES), P())
    out_specs = (P(AXES, None), P(AXES), P())
    return jax.shard_map(body, mesh=mesh, in_specs=in_specs, out_specs=out_specs, check_vma=False)
```

```python
import functools

import jax
import jax.numpy as jnp
from jax import lax
from jax.experimental import pallas as pl
from jax.experimental.pallas import tpu as pltpu
from jax.sharding import PartitionSpec as P

PMAX = 16
EPS = 1e-06
TAU = 6.0
RIDGE = 1.0
AXES = ("rows", "cols")
NDEV = 128
CLASSES = 8
RING = 4
SUB = 4
NORM_TILES = 14
SOLVE_SUB = 4
GRANT = 58 << 20
LOG2E = 1.4426950408889634
TILES = 8
BS = 32
F32 = jnp.float32
BF16 = jnp.bfloat16


def iota(shape, dim):
    return lax.broadcasted_iota(jnp.int32, shape, dim)


def learn(c):
    return (c * (16.0 - c) + 8.0) / 72.0


def own_kernel(
    dev_ref, piv_s, piv_v, solved_ref, emb_ref, fac_ref, send_ref, loc_ref, ebuf, fbuf, sem
):
    rows_here, dim = emb_ref.shape
    k0 = fac_ref.shape[1]
    total = piv_s.shape[0]
    first = dev_ref[0] * rows_here
    pv = piv_v[...]
    before = jnp.sum((pv < first).astype(F32)).astype(jnp.int32)
    upto = jnp.sum((pv < first + rows_here).astype(F32)).astype(jnp.int32)
    mine = upto - before
    loc_ref[0] = before
    loc_ref[1] = mine
    idx = []
    copies = []
    for s in range(PMAX):
        p = piv_s[jnp.minimum(before + s, total - 1)]
        i = jnp.clip(p - first, 0, rows_here - 1)
        loc_ref[2 + s] = i
        idx.append(i)
        base = pl.multiple_of((i // 16) * 16, 16)
        c1 = pltpu.make_async_copy(
            emb_ref.at[pl.ds(base, 16), :], ebuf.at[pl.ds(16 * s, 16), :], sem.at[0, s]
        )
        c2 = pltpu.make_async_copy(
            fac_ref.at[pl.ds(base, 16), :], fbuf.at[pl.ds(16 * s, 16), :], sem.at[1, s]
        )
        c1.start()
        c2.start()
        copies += [c1, c2]
    r = iota((16, 16 * PMAX), 0)
    q = iota((16, 16 * PMAX), 1)
    rc = iota((16, 128), 0)
    lane = iota((16, 128), 1)
    hot = jnp.zeros((16, 16 * PMAX), F32)
    tag = jnp.zeros((16, 128), F32)
    for s in range(PMAX):
        j = before + s
        row = jnp.where(s < mine, 2 * lax.rem(j, CLASSES) + s // CLASSES, -1)
        hot = jnp.where((r == row) & (q == 16 * s + lax.rem(idx[s], 16)), 1.0, hot)
        c = solved_ref[idx[s] // 128, lax.rem(idx[s], 128)].astype(F32)
        tag = jnp.where(rc == row, jnp.where(lane == 0, c, (j + 1).astype(F32)), tag)
    hot = hot.astype(BF16)
    for c in copies:
        c.wait()
    send_ref[:, 0:dim] = jnp.dot(hot, ebuf[...], preferred_element_type=F32).astype(BF16)
    send_ref[:, dim : dim + k0] = jnp.dot(hot, fbuf[...], preferred_element_type=F32).astype(BF16)
    send_ref[:, dim + k0 :] = tag.astype(BF16)


def slots_kernel(cls_ref, *refs):
    out = refs[-1]
    slots, width = out.shape
    data = jnp.concatenate([ref[...] for ref in refs[:-1]], axis=0)
    ids = data[:, width - 127 : width - 126].astype(F32)
    want = (CLASSES * iota((data.shape[0], slots), 1) + cls_ref[0] + 1).astype(F32)
    hot = (ids == want).astype(BF16)
    out[...] = lax.dot_general(
        hot, data, (((0,), (0,)), ((), ())), preferred_element_type=F32
    ).astype(BF16)


def norms_kernel(first, solved_ref, emb_hbm, fac_hbm, *refs):
    aux_hbm, emb_ref, fac_ref, aux_ref, sem, out_sem = refs[-6:]
    rows, dim = emb_ref.shape
    tile = emb_hbm.shape[0] // NORM_TILES
    nchunk = tile // 128
    ey = iota((128, 128), 0) == iota((128, 128), 1)
    lane = iota((128, 128), 1)
    ndims = (((1,), (1,)), ((), ()))

    def fetch(t):
        src = pl.ds(pl.multiple_of((first + t) * tile, tile), tile)
        dst = pl.ds(pl.multiple_of(t * tile, tile), tile)
        return [
            pltpu.make_async_copy(x.at[src, :], y.at[dst, :], sem.at[k, t])
            for k, (x, y) in enumerate(((emb_hbm, emb_ref), (fac_hbm, fac_ref)))
        ]

    def store(t):
        src = pl.ds(pl.multiple_of(t * tile, tile), tile)
        dst = pl.ds(pl.multiple_of((first + t) * tile, tile), tile)
        return pltpu.make_async_copy(aux_ref.at[src, :], aux_hbm.at[dst, :], out_sem.at[t])

    for t in range(rows // tile):
        for c in fetch(t):
            c.start()

    def step(t, carry):
        st = solved_ref[pl.ds((first + t) * nchunk, nchunk), :].astype(F32)
        for c in fetch(t):
            c.wait()
        for c in range(nchunk):
            o = pl.ds(pl.multiple_of(t * tile + 128 * c, 128), 128)
            x = emb_ref[o, :].astype(F32)
            f = fac_ref[o, :]
            ff = lax.dot_general(f, f, ndims, preferred_element_type=F32)
            ss = jnp.sum(x * x, axis=1, keepdims=True)
            fs = jnp.sum(jnp.where(ey, ff, 0.0), axis=1, keepdims=True)
            a = 1.0 / jnp.sqrt(ss / dim + EPS)
            b = jnp.broadcast_to(st[c : c + 1, :], (128, 128))
            q = learn(jnp.sum(jnp.where(ey, b, 0.0), axis=1, keepdims=True))
            aux_ref[o, :] = jnp.where(
                lane == 0, q * q + RIDGE - fs, jnp.where(lane == 1, a, q)
            )
        store(t).start()
        return carry

    lax.fori_loop(0, rows // tile, step, 0)
    for t in range(rows // tile):
        store(t).wait()


def split3(x):
    h = x.astype(BF16)
    r = x - h.astype(F32)
    m = r.astype(BF16)
    l = (r - m.astype(F32)).astype(BF16)
    return h, m, l


def lanes(x, k):
    return jnp.broadcast_to(x[:, k : k + 1], x.shape)


def sublanes(x, k):
    return jnp.broadcast_to(x[k : k + 1, :], x.shape)


def eliminate(w, between):
    rows, width = w.shape
    groups = [
        [w[8 * g : 8 * g + 8, 128 * v : 128 * v + 128] for v in range(width // 128)]
        for g in range(rows // 8)
    ]
    srow = iota((8, 128), 0)
    done = []
    for t in range(rows // 8):
        cols = [lanes(groups[t][0], 8 * t + k) for k in range(8)]
        e = [[sublanes(cols[k], i) for k in range(i + 1)] for i in range(8)]
        below = {
            g: [lanes(groups[g][0], 8 * t + k) for k in range(8)]
            for g in range(t + 1, rows // 8)
        }
        tops = [[sublanes(x, j) for x in groups[t]] for j in range(8)]
        m = [[None] * 8 for _ in range(8)]
        n = [[None] * 8 for _ in range(8)]
        for k in range(8):
            inv = 1.0 / e[k][k]
            for i in range(k + 1, 8):
                m[i][k] = e[i][k] * inv
                for j in range(k + 1, i + 1):
                    e[i][j] = e[i][j] - m[i][k] * e[j][k]
            for j in range(k):
                acc = m[k][j]
                for l in range(j + 1, k):
                    acc = acc + m[k][l] * n[l][j]
                n[k][j] = -acc
        root = [1.0 / jnp.sqrt(e[k][k]) for k in range(8)]
        inv = [[root[i] * n[i][j] for j in range(i)] + [root[i]] for i in range(8)]
        cols = []
        for j in range(8):
            c = jnp.where(srow == j, inv[j][j], 0.0)
            for i in range(j + 1, 8):
                c = jnp.where(srow == i, inv[i][j], c)
            cols.append(c)
        out = []
        for v in range(width // 128):
            acc = cols[0] * tops[0][v]
            for j in range(1, 8):
                acc = acc + cols[j] * tops[j][v]
            out.append(acc)
        for g in range(t + 1, rows // 8):
            for j in range(8):
                c = below[g][0] * inv[j][0]
                for k in range(1, j + 1):
                    c = c + below[g][k] * inv[j][k]
                groups[g] = [x - c * sublanes(o, j) for x, o in zip(groups[g], out)]
        done.append(jnp.concatenate(out, axis=1))
        between(t)
    return jnp.concatenate(done, axis=0)


def main_kernel(
    loc_ref, one_ref, two_ref, aux_hbm, emb_hbm, fac_hbm,
    out_hbm, gains_ref, best_ref,
    piv, pvec, ar, minv, mt, panel, aux_ref, emb_ref, fac_ref, out_ref, raw_a, raw_b, sem, out_sem,
):
    rows_here, dim = emb_ref.shape
    tile = rows_here // TILES
    k0 = fac_ref.shape[1]
    n = piv.shape[0]

    def fetch(t):
        w = pl.ds(pl.multiple_of(t * tile, tile), tile)
        return [
            pltpu.make_async_copy(src.at[w, :], dst.at[w, :], sem.at[k, t])
            for k, (src, dst) in enumerate(
                ((aux_hbm, aux_ref), (emb_hbm, emb_ref), (fac_hbm, fac_ref))
            )
        ]

    for t in range(TILES):
        for c in fetch(t):
            c.start()

    nchunk = tile // 128
    sub = tile // SUB
    tdims = (((0,), (0,)), ((), ()))
    ndims = (((1,), (1,)), ((), ()))

    jj = iota((n, n), 0)
    qq = iota((n, n), 1)
    eye = (jj == qq).astype(F32)
    data = jnp.concatenate([one_ref[...], two_ref[...]], axis=0)
    ids = data[:, dim + k0 + 1 : dim + k0 + 2].astype(F32)
    permt = (ids == (qq + 1).astype(F32)).astype(BF16)
    v = lax.dot_general(permt, data, tdims, preferred_element_type=F32)
    pb = v.astype(BF16)
    piv[...] = pb[:, 0 : dim + k0]
    cs = 1.0 / jnp.sqrt(
        jnp.sum(v[:, 0:dim] * v[:, 0:dim], axis=1, keepdims=True) / dim + EPS
    )
    cq = learn(v[:, dim + k0 : dim + k0 + 1])
    rs = jnp.sum(eye * cs, axis=0, keepdims=True) * (TAU * LOG2E / dim)
    rq = jnp.sum(eye * cq, axis=0, keepdims=True)
    pvec[0:1, :] = rs
    pvec[1:2, :] = rq
    dots = lax.dot_general(pb[:, 0:dim], piv[:, 0:dim], ndims, preferred_element_type=F32)
    shared = lax.dot_general(
        pb[:, dim : dim + k0], piv[:, dim : dim + k0], ndims, preferred_element_type=F32
    )
    similar = jnp.exp2(dots * (cs * rs) - TAU * LOG2E)
    ar[:, 0:n] = similar * (cq * rq) + RIDGE * eye - shared
    ar[:, n : 2 * n] = eye

    def step(i, carry):
        for c in fetch(i):
            c.wait()
        def part_of_panel(c):
            w = pl.ds(pl.multiple_of(i * tile + sub * c, 16), sub)
            a = aux_ref[w, 1:2]
            q = aux_ref[w, 2:3]
            dots = lax.dot_general(
                emb_ref[w, :], piv[:, 0:dim], ndims, preferred_element_type=F32
            )
            shared = lax.dot_general(
                fac_ref[w, :], piv[:, dim : dim + k0], ndims, preferred_element_type=F32
            )
            similar = jnp.exp2(dots * (a * pvec[0:1, :]) - TAU * LOG2E)
            p = similar * (q * pvec[1:2, :]) - shared
            ph = p.astype(BF16)
            panel[w, 0:n] = ph
            panel[w, n : 2 * n] = (p - ph.astype(F32)).astype(BF16)

        rows = pl.ds(pl.multiple_of(i * BS, BS), BS)
        shift = lax.rem(n - i * BS, n)
        a = pltpu.roll(ar[rows, 0:n], shift, 1)
        w = eliminate(jnp.concatenate([a, ar[rows, n : 2 * n]], axis=1), part_of_panel)
        u = pltpu.roll(w[:, 0:n], i * BS, 1)
        m = w[:, n : 2 * n]
        minv[rows, :] = m
        uh, um, ul = split3(u)
        mh, mm, ml = split3(m)
        left = jnp.concatenate([uh, uh, um, uh, ul, um], axis=0)
        r_a = jnp.concatenate([uh, um, uh, ul, uh, um], axis=0)
        r_m = jnp.concatenate([mh, mm, mh, ml, mh, mm], axis=0)
        ar[:, 0:n] -= lax.dot_general(left, r_a, tdims, preferred_element_type=F32)
        ar[:, n : 2 * n] -= lax.dot_general(left, r_m, tdims, preferred_element_type=F32)
        return carry

    lax.fori_loop(0, TILES, step, 0)

    t = minv[...].T
    h = t.astype(BF16)
    mt[0:n, :] = h
    mt[n : 2 * n, :] = h
    mt[2 * n : 3 * n, :] = (t - h.astype(F32)).astype(BF16)
    best_ref[...] = jnp.full(best_ref.shape, -jnp.inf, F32)

    def ridge(s, carry):
        at = loc_ref[2 + s]
        w = pl.ds(pl.multiple_of((at // 16) * 16, 16), 16)
        p = panel[w, 0:n].astype(F32) + panel[w, n : 2 * n].astype(F32)
        here = (iota((16, n), 0) == lax.rem(at, 16)) & (iota((16, n), 1) == loc_ref[0] + s)
        p = p + jnp.where(here, RIDGE, 0.0)
        ph = p.astype(BF16)
        panel[w, 0:n] = ph
        panel[w, n : 2 * n] = (p - ph.astype(F32)).astype(BF16)
        return carry

    lax.fori_loop(0, jnp.minimum(loc_ref[1], PMAX), ridge, 0)

    def store(t):
        w = pl.ds(pl.multiple_of(t * tile, tile), tile)
        return pltpu.make_async_copy(out_ref.at[w, :], out_hbm.at[w, :], out_sem.at[t])

    part = tile // SOLVE_SUB
    ey = iota((128, 128), 0) == iota((128, 128), 1)

    def product(t, raw):
        for c in range(SOLVE_SUB):
            w = pl.ds(pl.multiple_of(t * tile + part * c, 16), part)
            both = jnp.concatenate([panel[w, :], panel[w, 0:n]], axis=1)
            raw[part * c : part * c + part, :] = jnp.dot(
                both, mt[...], preferred_element_type=F32
            )

    def finish(t, raw):
        lines = []
        for c in range(nchunk):
            full = raw[128 * c : 128 * c + 128, :]
            w = pl.ds(pl.multiple_of(t * tile + 128 * c, 128), 128)
            out_ref[w, :] = full.astype(BF16)
            g = aux_ref[w, 0:1] - jnp.sum(full * full, axis=1, keepdims=True)
            b = jnp.broadcast_to(g, (128, 128))
            lines.append(jnp.sum(jnp.where(ey, b, 0.0), axis=0, keepdims=True))
        lines = jnp.concatenate(lines, axis=0)
        gains_ref[pl.ds(t * nchunk, nchunk), :] = lines
        best_ref[...] = jnp.maximum(best_ref[...], jnp.max(lines, axis=0, keepdims=True))

    product(0, raw_a)

    def solve(t, carry):
        product(2 * t + 1, raw_b)
        finish(2 * t, raw_a)
        product(2 * t + 2, raw_a)
        finish(2 * t + 1, raw_b)
        store(2 * t).start()
        store(2 * t + 1).start()
        return carry

    lax.fori_loop(0, TILES // 2 - 1, solve, 0)
    product(TILES - 1, raw_b)
    finish(TILES - 2, raw_a)
    store(TILES - 2).start()
    finish(TILES - 1, raw_b)
    store(TILES - 1).start()
    for t in range(TILES):
        store(t).wait()


def main_call(loc, one, two, aux, embeddings, factor_cols):
    rows_here, dim = embeddings.shape
    k0 = factor_cols.shape[1]
    total = one.shape[0] + two.shape[0]
    tile = rows_here // TILES
    smem = pl.BlockSpec(memory_space=pltpu.SMEM)
    vmem = pl.BlockSpec(memory_space=pltpu.VMEM)
    hbm = pl.BlockSpec(memory_space=pltpu.HBM)
    return pl.pallas_call(
        main_kernel,
        out_shape=(
            jax.ShapeDtypeStruct((rows_here, total), BF16),
            jax.ShapeDtypeStruct((rows_here // 128, 128), F32),
            jax.ShapeDtypeStruct((NDEV, 128), F32),
        ),
        in_specs=[smem, vmem, vmem, hbm, hbm, hbm],
        out_specs=(hbm, vmem, vmem),
        scratch_shapes=[
            pltpu.VMEM((total, dim + k0), BF16),
            pltpu.VMEM((8, total), F32),
            pltpu.VMEM((total, 2 * total), F32),
            pltpu.VMEM((total, total), F32),
            pltpu.VMEM((3 * total, total), BF16),
            pltpu.VMEM((rows_here, 2 * total), BF16),
            pltpu.VMEM((rows_here, 128), F32),
            pltpu.VMEM((rows_here, dim), BF16),
            pltpu.VMEM((rows_here, k0), BF16),
            pltpu.VMEM((rows_here, total), BF16),
            pltpu.VMEM((tile, total), F32),
            pltpu.VMEM((tile, total), F32),
            pltpu.SemaphoreType.DMA((3, TILES)),
            pltpu.SemaphoreType.DMA((TILES,)),
        ],
        compiler_params=pltpu.CompilerParams(vmem_limit_bytes=GRANT),
        name="panel_factor",
    )(loc, one, two, aux, embeddings, factor_cols)


def norms_part(solved2, embeddings, factor_cols, first, last, aux):
    rows_here, dim = embeddings.shape
    k0 = factor_cols.shape[1]
    tile = rows_here // NORM_TILES
    rows = (last - first) * tile
    hbm = pl.BlockSpec(memory_space=pltpu.HBM)
    specs = [pl.BlockSpec(memory_space=pltpu.VMEM), hbm, hbm]
    args = (solved2, embeddings, factor_cols)
    if aux is not None:
        specs.append(hbm)
        args += (aux,)
    return pl.pallas_call(
        functools.partial(norms_kernel, first),
        out_shape=jax.ShapeDtypeStruct((rows_here, 128), F32),
        in_specs=specs,
        out_specs=hbm,
        scratch_shapes=[
            pltpu.VMEM((rows, dim), BF16),
            pltpu.VMEM((rows, k0), BF16),
            pltpu.VMEM((rows, 128), F32),
            pltpu.SemaphoreType.DMA((2, last - first)),
            pltpu.SemaphoreType.DMA((last - first,)),
        ],
        input_output_aliases={} if aux is None else {3: 0},
        compiler_params=pltpu.CompilerParams(vmem_limit_bytes=GRANT),
        cost_estimate=pl.CostEstimate(
            flops=rows * (dim + k0) * 4, bytes_accessed=rows * (dim + k0) * 2, transcendentals=0
        ),
        name="row_norms",
    )(*args)


def ring(values, axis, pairs):
    return [lax.ppermute(v, axis, p) for v, p in zip(values, pairs)]


def body(embeddings, factor_cols, solved, pivots):
    rows_here, dim = embeddings.shape
    k0 = factor_cols.shape[1]
    total = pivots.shape[0]
    width = dim + k0 + 128
    tile = rows_here // TILES
    r = lax.axis_index("rows").astype(jnp.int32)
    c = lax.axis_index("cols").astype(jnp.int32)
    dev = (r * 16 + c).reshape(1)
    solved2 = solved.reshape(rows_here // 128, 128)
    piv2 = pivots.reshape(total // 128, 128)
    smem = pl.BlockSpec(memory_space=pltpu.SMEM)
    vmem = pl.BlockSpec(memory_space=pltpu.VMEM)
    hbm = pl.BlockSpec(memory_space=pltpu.HBM)
    small = pltpu.CompilerParams(vmem_limit_bytes=8 << 20)
    wide = lambda rows: jax.ShapeDtypeStruct((rows, width), BF16)
    swap = [(i, i ^ 1) for i in range(8)]
    zs = [[(i, i ^ (2 * k)) for i in range(8)] for k in range(1, RING)]
    xs = [[(i, i ^ (4 * k)) for i in range(16)] for k in range(1, RING)]
    ys = [[(i, i ^ k) for i in range(16)] for k in range(1, RING)]

    send, loc = pl.pallas_call(
        own_kernel,
        out_shape=(wide(16), jax.ShapeDtypeStruct((2 + PMAX,), jnp.int32)),
        in_specs=[smem, smem, vmem, smem, hbm, hbm],
        out_specs=(vmem, smem),
        scratch_shapes=[
            pltpu.VMEM((16 * PMAX, dim), BF16),
            pltpu.VMEM((16 * PMAX, k0), BF16),
            pltpu.SemaphoreType.DMA((2, PMAX)),
        ],
        compiler_params=pltpu.CompilerParams(vmem_limit_bytes=GRANT),
        name="own_rows",
    )(dev, pivots, piv2, solved2, embeddings, factor_cols)
    mine = lax.all_to_all(send.reshape(CLASSES, 2, width), "rows", 0, 0).reshape(16, width)
    counts, mine = lax.optimization_barrier((solved2, mine))
    got = [mine] + ring([mine] * 3, "cols", xs)
    aux = norms_part(counts, embeddings, factor_cols, 0, 5, None)
    aux, *got = lax.optimization_barrier((aux, *got))
    mine = pl.pallas_call(
        slots_kernel,
        out_shape=wide(total // CLASSES),
        in_specs=[smem] + [vmem] * RING,
        out_specs=vmem,
        compiler_params=small,
        name="slots",
    )(r.reshape(1), *got)
    counts, mine = lax.optimization_barrier((solved2, mine))
    got = [mine] + ring([mine] * 3, "cols", ys)
    aux = norms_part(counts, embeddings, factor_cols, 5, 10, aux)
    aux, *got = lax.optimization_barrier((aux, *got))
    mine = got[0] + got[1] + got[2] + got[3]
    counts, mine = lax.optimization_barrier((solved2, mine))
    got = [mine] + ring([mine] * 3, "rows", zs)
    aux = norms_part(counts, embeddings, factor_cols, 10, NORM_TILES, aux)
    aux, *got = lax.optimization_barrier((aux, *got))
    one = jnp.concatenate(got, axis=0)
    two = lax.ppermute(one, "rows", swap)

    new_cols, gains, best = main_call(loc, one, two, aux, embeddings, factor_cols)
    peers = lax.all_to_all(best.reshape(NDEV, 1, 128), AXES, 0, 0)
    return new_cols, gains.reshape(rows_here), jnp.max(peers)


def solution(mesh):
    in_specs = (P(AXES, None), P(AXES, None), P(AXES), P())
    out_specs = (P(AXES, None), P(AXES), P())
    return jax.shard_map(body, mesh=mesh, in_specs=in_specs, out_specs=out_specs, check_vma=False)
```

```python
import functools

import jax
import jax.numpy as jnp
from jax import lax
from jax.experimental import pallas as pl
from jax.experimental.pallas import tpu as pltpu
from jax.sharding import PartitionSpec as P

PMAX = 16
EPS = 1e-06
TAU = 6.0
RIDGE = 1.0
AXES = ("rows", "cols")
NDEV = 128
CLASSES = 8
RING = 4
SUB = 4
NORM_TILES = 14
SOLVE_SUB = 4
GRANT = 58 << 20
LOG2E = 1.4426950408889634
TILES = 8
BS = 32
F32 = jnp.float32
BF16 = jnp.bfloat16


def iota(shape, dim):
    return lax.broadcasted_iota(jnp.int32, shape, dim)


def learn(c):
    return (c * (16.0 - c) + 8.0) / 72.0


def own_kernel(
    dev_ref, piv_s, piv_v, solved_ref, emb_ref, fac_ref, send_ref, loc_ref, ebuf, fbuf, sem
):
    rows_here, dim = emb_ref.shape
    k0 = fac_ref.shape[1]
    total = piv_s.shape[0]
    first = dev_ref[0] * rows_here
    pv = piv_v[...]
    before = jnp.sum((pv < first).astype(F32)).astype(jnp.int32)
    upto = jnp.sum((pv < first + rows_here).astype(F32)).astype(jnp.int32)
    mine = upto - before
    loc_ref[0] = before
    loc_ref[1] = mine
    idx = []
    copies = []
    for s in range(PMAX):
        p = piv_s[jnp.minimum(before + s, total - 1)]
        i = jnp.clip(p - first, 0, rows_here - 1)
        loc_ref[2 + s] = i
        idx.append(i)
        base = pl.multiple_of((i // 16) * 16, 16)
        c1 = pltpu.make_async_copy(
            emb_ref.at[pl.ds(base, 16), :], ebuf.at[pl.ds(16 * s, 16), :], sem.at[0, s]
        )
        c2 = pltpu.make_async_copy(
            fac_ref.at[pl.ds(base, 16), :], fbuf.at[pl.ds(16 * s, 16), :], sem.at[1, s]
        )
        c1.start()
        c2.start()
        copies += [c1, c2]
    r = iota((16, 16 * PMAX), 0)
    q = iota((16, 16 * PMAX), 1)
    rc = iota((16, 128), 0)
    lane = iota((16, 128), 1)
    hot = jnp.zeros((16, 16 * PMAX), F32)
    tag = jnp.zeros((16, 128), F32)
    for s in range(PMAX):
        j = before + s
        row = jnp.where(s < mine, 2 * lax.rem(j, CLASSES) + s // CLASSES, -1)
        hot = jnp.where((r == row) & (q == 16 * s + lax.rem(idx[s], 16)), 1.0, hot)
        c = solved_ref[idx[s] // 128, lax.rem(idx[s], 128)].astype(F32)
        tag = jnp.where(rc == row, jnp.where(lane == 0, c, (j + 1).astype(F32)), tag)
    hot = hot.astype(BF16)
    for c in copies:
        c.wait()
    e = jnp.dot(hot, ebuf[...], preferred_element_type=F32)
    f = jnp.dot(hot, fbuf[...], preferred_element_type=F32)
    row = jnp.concatenate([e, f, tag], axis=1)
    for k in range(CLASSES):
        send_ref[k, :, :] = row[2 * k : 2 * k + 2, :].astype(BF16)


def slots_kernel(cls_ref, *refs):
    out = refs[-1]
    slots, width = out.shape
    data = jnp.concatenate([ref[...] for ref in refs[:-1]], axis=0)
    ids = data[:, width - 127 : width - 126].astype(F32)
    want = (CLASSES * iota((data.shape[0], slots), 1) + cls_ref[0] + 1).astype(F32)
    hot = (ids == want).astype(BF16)
    out[...] = lax.dot_general(
        hot, data, (((0,), (0,)), ((), ())), preferred_element_type=F32
    ).astype(BF16)


def norms_kernel(first, solved_ref, emb_hbm, fac_hbm, *refs):
    aux_hbm, emb_ref, fac_ref, aux_ref, sem, out_sem = refs[-6:]
    rows, dim = emb_ref.shape
    tile = emb_hbm.shape[0] // NORM_TILES
    nchunk = tile // 128
    ey = iota((128, 128), 0) == iota((128, 128), 1)
    lane = iota((128, 128), 1)
    ndims = (((1,), (1,)), ((), ()))

    def fetch(t):
        src = pl.ds(pl.multiple_of((first + t) * tile, tile), tile)
        dst = pl.ds(pl.multiple_of(t * tile, tile), tile)
        return [
            pltpu.make_async_copy(x.at[src, :], y.at[dst, :], sem.at[k, t])
            for k, (x, y) in enumerate(((emb_hbm, emb_ref), (fac_hbm, fac_ref)))
        ]

    def store(t):
        src = pl.ds(pl.multiple_of(t * tile, tile), tile)
        dst = pl.ds(pl.multiple_of((first + t) * tile, tile), tile)
        return pltpu.make_async_copy(aux_ref.at[src, :], aux_hbm.at[dst, :], out_sem.at[t])

    for t in range(rows // tile):
        for c in fetch(t):
            c.start()

    def step(t, carry):
        st = solved_ref[pl.ds((first + t) * nchunk, nchunk), :].astype(F32)
        for c in fetch(t):
            c.wait()
        for c in range(nchunk):
            o = pl.ds(pl.multiple_of(t * tile + 128 * c, 128), 128)
            x = emb_ref[o, :].astype(F32)
            f = fac_ref[o, :]
            ff = lax.dot_general(f, f, ndims, preferred_element_type=F32)
            ss = jnp.sum(x * x, axis=1, keepdims=True)
            fs = jnp.sum(jnp.where(ey, ff, 0.0), axis=1, keepdims=True)
            a = 1.0 / jnp.sqrt(ss / dim + EPS)
            b = jnp.broadcast_to(st[c : c + 1, :], (128, 128))
            q = learn(jnp.sum(jnp.where(ey, b, 0.0), axis=1, keepdims=True))
            aux_ref[o, :] = jnp.where(
                lane == 0, q * q + RIDGE - fs, jnp.where(lane == 1, a, q)
            )
        store(t).start()
        return carry

    lax.fori_loop(0, rows // tile, step, 0)
    for t in range(rows // tile):
        store(t).wait()


def split3(x):
    h = x.astype(BF16)
    r = x - h.astype(F32)
    m = r.astype(BF16)
    l = (r - m.astype(F32)).astype(BF16)
    return h, m, l


def lanes(x, k):
    return jnp.broadcast_to(x[:, k : k + 1], x.shape)


def sublanes(x, k):
    return jnp.broadcast_to(x[k : k + 1, :], x.shape)


def eliminate(w, between):
    rows, width = w.shape
    groups = [
        [w[8 * g : 8 * g + 8, 128 * v : 128 * v + 128] for v in range(width // 128)]
        for g in range(rows // 8)
    ]
    srow = iota((8, 128), 0)
    done = []
    for t in range(rows // 8):
        cols = [lanes(groups[t][0], 8 * t + k) for k in range(8)]
        e = [[sublanes(cols[k], i) for k in range(i + 1)] for i in range(8)]
        below = {
            g: [lanes(groups[g][0], 8 * t + k) for k in range(8)]
            for g in range(t + 1, rows // 8)
        }
        tops = [[sublanes(x, j) for x in groups[t]] for j in range(8)]
        m = [[None] * 8 for _ in range(8)]
        n = [[None] * 8 for _ in range(8)]
        for k in range(8):
            inv = 1.0 / e[k][k]
            for i in range(k + 1, 8):
                m[i][k] = e[i][k] * inv
                for j in range(k + 1, i + 1):
                    e[i][j] = e[i][j] - m[i][k] * e[j][k]
            for j in range(k):
                acc = m[k][j]
                for l in range(j + 1, k):
                    acc = acc + m[k][l] * n[l][j]
                n[k][j] = -acc
        root = [1.0 / jnp.sqrt(e[k][k]) for k in range(8)]
        inv = [[root[i] * n[i][j] for j in range(i)] + [root[i]] for i in range(8)]
        cols = []
        for j in range(8):
            c = jnp.where(srow == j, inv[j][j], 0.0)
            for i in range(j + 1, 8):
                c = jnp.where(srow == i, inv[i][j], c)
            cols.append(c)
        out = []
        for v in range(width // 128):
            acc = cols[0] * tops[0][v]
            for j in range(1, 8):
                acc = acc + cols[j] * tops[j][v]
            out.append(acc)
        for g in range(t + 1, rows // 8):
            for j in range(8):
                c = below[g][0] * inv[j][0]
                for k in range(1, j + 1):
                    c = c + below[g][k] * inv[j][k]
                groups[g] = [x - c * sublanes(o, j) for x, o in zip(groups[g], out)]
        done.append(jnp.concatenate(out, axis=1))
        between(t)
    return jnp.concatenate(done, axis=0)


def main_kernel(
    loc_ref, one_ref, two_ref, aux_hbm, emb_hbm, fac_hbm,
    out_hbm, gains_ref, best_ref,
    piv, pvec, ar, minv, mt, panel, aux_ref, emb_ref, fac_ref, out_ref, raw_a, raw_b, sem, out_sem,
):
    rows_here, dim = emb_ref.shape
    tile = rows_here // TILES
    k0 = fac_ref.shape[1]
    n = piv.shape[0]

    def fetch(t):
        w = pl.ds(pl.multiple_of(t * tile, tile), tile)
        return [
            pltpu.make_async_copy(src.at[w, :], dst.at[w, :], sem.at[k, t])
            for k, (src, dst) in enumerate(
                ((aux_hbm, aux_ref), (emb_hbm, emb_ref), (fac_hbm, fac_ref))
            )
        ]

    for t in range(TILES):
        for c in fetch(t):
            c.start()

    nchunk = tile // 128
    sub = tile // SUB
    tdims = (((0,), (0,)), ((), ()))
    ndims = (((1,), (1,)), ((), ()))

    jj = iota((n, n), 0)
    qq = iota((n, n), 1)
    eye = (jj == qq).astype(F32)
    data = jnp.concatenate([one_ref[...], two_ref[...]], axis=0)
    ids = data[:, dim + k0 + 1 : dim + k0 + 2].astype(F32)
    permt = (ids == (qq + 1).astype(F32)).astype(BF16)
    v = lax.dot_general(permt, data, tdims, preferred_element_type=F32)
    pb = v.astype(BF16)
    piv[...] = pb[:, 0 : dim + k0]
    cs = 1.0 / jnp.sqrt(
        jnp.sum(v[:, 0:dim] * v[:, 0:dim], axis=1, keepdims=True) / dim + EPS
    )
    cq = learn(v[:, dim + k0 : dim + k0 + 1])
    rs = jnp.sum(eye * cs, axis=0, keepdims=True) * (TAU * LOG2E / dim)
    rq = jnp.sum(eye * cq, axis=0, keepdims=True)
    pvec[0:1, :] = rs
    pvec[1:2, :] = rq
    dots = lax.dot_general(pb[:, 0:dim], piv[:, 0:dim], ndims, preferred_element_type=F32)
    shared = lax.dot_general(
        pb[:, dim : dim + k0], piv[:, dim : dim + k0], ndims, preferred_element_type=F32
    )
    similar = jnp.exp2(dots * (cs * rs) - TAU * LOG2E)
    ar[:, 0:n] = similar * (cq * rq) + RIDGE * eye - shared
    ar[:, n : 2 * n] = eye

    def step(i, carry):
        for c in fetch(i):
            c.wait()
        def part_of_panel(c):
            w = pl.ds(pl.multiple_of(i * tile + sub * c, 16), sub)
            a = aux_ref[w, 1:2]
            q = aux_ref[w, 2:3]
            dots = lax.dot_general(
                emb_ref[w, :], piv[:, 0:dim], ndims, preferred_element_type=F32
            )
            shared = lax.dot_general(
                fac_ref[w, :], piv[:, dim : dim + k0], ndims, preferred_element_type=F32
            )
            similar = jnp.exp2(dots * (a * pvec[0:1, :]) - TAU * LOG2E)
            p = similar * (q * pvec[1:2, :]) - shared
            ph = p.astype(BF16)
            panel[w, 0:n] = ph
            panel[w, n : 2 * n] = (p - ph.astype(F32)).astype(BF16)

        rows = pl.ds(pl.multiple_of(i * BS, BS), BS)
        shift = lax.rem(n - i * BS, n)
        a = pltpu.roll(ar[rows, 0:n], shift, 1)
        w = eliminate(jnp.concatenate([a, ar[rows, n : 2 * n]], axis=1), part_of_panel)
        u = pltpu.roll(w[:, 0:n], i * BS, 1)
        m = w[:, n : 2 * n]
        minv[rows, :] = m
        uh, um, ul = split3(u)
        mh, mm, ml = split3(m)
        left = jnp.concatenate([uh, uh, um, uh, ul, um], axis=0)
        r_a = jnp.concatenate([uh, um, uh, ul, uh, um], axis=0)
        r_m = jnp.concatenate([mh, mm, mh, ml, mh, mm], axis=0)
        ar[:, 0:n] -= lax.dot_general(left, r_a, tdims, preferred_element_type=F32)
        ar[:, n : 2 * n] -= lax.dot_general(left, r_m, tdims, preferred_element_type=F32)
        return carry

    lax.fori_loop(0, TILES, step, 0)

    t = minv[...].T
    h = t.astype(BF16)
    mt[0:n, :] = h
    mt[n : 2 * n, :] = h
    mt[2 * n : 3 * n, :] = (t - h.astype(F32)).astype(BF16)
    best_ref[...] = jnp.full(best_ref.shape, -jnp.inf, F32)

    def ridge(s, carry):
        at = loc_ref[2 + s]
        w = pl.ds(pl.multiple_of((at // 16) * 16, 16), 16)
        p = panel[w, 0:n].astype(F32) + panel[w, n : 2 * n].astype(F32)
        here = (iota((16, n), 0) == lax.rem(at, 16)) & (iota((16, n), 1) == loc_ref[0] + s)
        p = p + jnp.where(here, RIDGE, 0.0)
        ph = p.astype(BF16)
        panel[w, 0:n] = ph
        panel[w, n : 2 * n] = (p - ph.astype(F32)).astype(BF16)
        return carry

    lax.fori_loop(0, jnp.minimum(loc_ref[1], PMAX), ridge, 0)

    def store(t):
        w = pl.ds(pl.multiple_of(t * tile, tile), tile)
        return pltpu.make_async_copy(out_ref.at[w, :], out_hbm.at[w, :], out_sem.at[t])

    part = tile // SOLVE_SUB
    ey = iota((128, 128), 0) == iota((128, 128), 1)

    def product(t, raw):
        for c in range(SOLVE_SUB):
            w = pl.ds(pl.multiple_of(t * tile + part * c, 16), part)
            both = jnp.concatenate([panel[w, :], panel[w, 0:n]], axis=1)
            raw[part * c : part * c + part, :] = jnp.dot(
                both, mt[...], preferred_element_type=F32
            )

    def finish(t, raw):
        lines = []
        for c in range(nchunk):
            full = raw[128 * c : 128 * c + 128, :]
            w = pl.ds(pl.multiple_of(t * tile + 128 * c, 128), 128)
            out_ref[w, :] = full.astype(BF16)
            g = aux_ref[w, 0:1] - jnp.sum(full * full, axis=1, keepdims=True)
            b = jnp.broadcast_to(g, (128, 128))
            lines.append(jnp.sum(jnp.where(ey, b, 0.0), axis=0, keepdims=True))
        lines = jnp.concatenate(lines, axis=0)
        gains_ref[pl.ds(t * nchunk, nchunk), :] = lines
        best_ref[...] = jnp.maximum(best_ref[...], jnp.max(lines, axis=0, keepdims=True))

    product(0, raw_a)

    def solve(t, carry):
        product(2 * t + 1, raw_b)
        finish(2 * t, raw_a)
        product(2 * t + 2, raw_a)
        finish(2 * t + 1, raw_b)
        store(2 * t).start()
        store(2 * t + 1).start()
        return carry

    lax.fori_loop(0, TILES // 2 - 1, solve, 0)
    product(TILES - 1, raw_b)
    finish(TILES - 2, raw_a)
    store(TILES - 2).start()
    finish(TILES - 1, raw_b)
    store(TILES - 1).start()
    for t in range(TILES):
        store(t).wait()


def main_call(loc, one, two, aux, embeddings, factor_cols):
    rows_here, dim = embeddings.shape
    k0 = factor_cols.shape[1]
    total = one.shape[0] + two.shape[0]
    tile = rows_here // TILES
    smem = pl.BlockSpec(memory_space=pltpu.SMEM)
    vmem = pl.BlockSpec(memory_space=pltpu.VMEM)
    hbm = pl.BlockSpec(memory_space=pltpu.HBM)
    return pl.pallas_call(
        main_kernel,
        out_shape=(
            jax.ShapeDtypeStruct((rows_here, total), BF16),
            jax.ShapeDtypeStruct((rows_here // 128, 128), F32),
            jax.ShapeDtypeStruct((NDEV, 128), F32),
        ),
        in_specs=[smem, vmem, vmem, hbm, hbm, hbm],
        out_specs=(hbm, vmem, vmem),
        scratch_shapes=[
            pltpu.VMEM((total, dim + k0), BF16),
            pltpu.VMEM((8, total), F32),
            pltpu.VMEM((total, 2 * total), F32),
            pltpu.VMEM((total, total), F32),
            pltpu.VMEM((3 * total, total), BF16),
            pltpu.VMEM((rows_here, 2 * total), BF16),
            pltpu.VMEM((rows_here, 128), F32),
            pltpu.VMEM((rows_here, dim), BF16),
            pltpu.VMEM((rows_here, k0), BF16),
            pltpu.VMEM((rows_here, total), BF16),
            pltpu.VMEM((tile, total), F32),
            pltpu.VMEM((tile, total), F32),
            pltpu.SemaphoreType.DMA((3, TILES)),
            pltpu.SemaphoreType.DMA((TILES,)),
        ],
        compiler_params=pltpu.CompilerParams(vmem_limit_bytes=50 << 20),
        name="panel_factor",
    )(loc, one, two, aux, embeddings, factor_cols)


def norms_part(solved2, embeddings, factor_cols, first, last, aux):
    rows_here, dim = embeddings.shape
    k0 = factor_cols.shape[1]
    tile = rows_here // NORM_TILES
    rows = (last - first) * tile
    hbm = pl.BlockSpec(memory_space=pltpu.HBM)
    specs = [pl.BlockSpec(memory_space=pltpu.VMEM), hbm, hbm]
    args = (solved2, embeddings, factor_cols)
    if aux is not None:
        specs.append(hbm)
        args += (aux,)
    return pl.pallas_call(
        functools.partial(norms_kernel, first),
        out_shape=jax.ShapeDtypeStruct((rows_here, 128), F32),
        in_specs=specs,
        out_specs=hbm,
        scratch_shapes=[
            pltpu.VMEM((rows, dim), BF16),
            pltpu.VMEM((rows, k0), BF16),
            pltpu.VMEM((rows, 128), F32),
            pltpu.SemaphoreType.DMA((2, last - first)),
            pltpu.SemaphoreType.DMA((last - first,)),
        ],
        input_output_aliases={} if aux is None else {3: 0},
        compiler_params=pltpu.CompilerParams(vmem_limit_bytes=GRANT),
        cost_estimate=pl.CostEstimate(
            flops=rows * (dim + k0) * 4, bytes_accessed=rows * (dim + k0) * 2, transcendentals=0
        ),
        name="row_norms",
    )(*args)


def ring(values, axis, pairs):
    return [lax.ppermute(v, axis, p) for v, p in zip(values, pairs)]


def body(embeddings, factor_cols, solved, pivots):
    rows_here, dim = embeddings.shape
    k0 = factor_cols.shape[1]
    total = pivots.shape[0]
    width = dim + k0 + 128
    tile = rows_here // TILES
    r = lax.axis_index("rows").astype(jnp.int32)
    c = lax.axis_index("cols").astype(jnp.int32)
    dev = (r * 16 + c).reshape(1)
    solved2 = solved.reshape(rows_here // 128, 128)
    piv2 = pivots.reshape(total // 128, 128)
    smem = pl.BlockSpec(memory_space=pltpu.SMEM)
    vmem = pl.BlockSpec(memory_space=pltpu.VMEM)
    hbm = pl.BlockSpec(memory_space=pltpu.HBM)
    small = pltpu.CompilerParams(vmem_limit_bytes=8 << 20)
    wide = lambda rows: jax.ShapeDtypeStruct((rows, width), BF16)
    swap = [(i, i ^ 1) for i in range(8)]
    zs = [[(i, i ^ (2 * k)) for i in range(8)] for k in range(1, RING)]
    xs = [[(i, i ^ (4 * k)) for i in range(16)] for k in range(1, RING)]
    ys = [[(i, i ^ k) for i in range(16)] for k in range(1, RING)]

    send, loc = pl.pallas_call(
        own_kernel,
        out_shape=(
            jax.ShapeDtypeStruct((CLASSES, 2, width), BF16),
            jax.ShapeDtypeStruct((2 + PMAX,), jnp.int32),
        ),
        in_specs=[smem, smem, vmem, smem, hbm, hbm],
        out_specs=(vmem, smem),
        scratch_shapes=[
            pltpu.VMEM((16 * PMAX, dim), BF16),
            pltpu.VMEM((16 * PMAX, k0), BF16),
            pltpu.SemaphoreType.DMA((2, PMAX)),
        ],
        compiler_params=pltpu.CompilerParams(vmem_limit_bytes=GRANT),
        name="own_rows",
    )(dev, pivots, piv2, solved2, embeddings, factor_cols)
    mine = lax.all_to_all(send, "rows", 0, 0).reshape(16, width)
    counts, mine = lax.optimization_barrier((solved2, mine))
    got = [mine] + ring([mine] * 3, "cols", xs)
    aux = norms_part(counts, embeddings, factor_cols, 0, 5, None)
    aux, *got = lax.optimization_barrier((aux, *got))
    mine = pl.pallas_call(
        slots_kernel,
        out_shape=wide(total // CLASSES),
        in_specs=[smem] + [vmem] * RING,
        out_specs=vmem,
        compiler_params=small,
        name="slots",
    )(r.reshape(1), *got)
    counts, mine = lax.optimization_barrier((solved2, mine))
    got = [mine] + ring([mine] * 3, "cols", ys)
    aux = norms_part(counts, embeddings, factor_cols, 5, 10, aux)
    aux, *got = lax.optimization_barrier((aux, *got))
    mine = got[0] + got[1] + got[2] + got[3]
    counts, mine = lax.optimization_barrier((solved2, mine))
    got = [mine] + ring([mine] * 3, "rows", zs)
    aux = norms_part(counts, embeddings, factor_cols, 10, NORM_TILES, aux)
    aux, *got = lax.optimization_barrier((aux, *got))
    one = jnp.concatenate(got, axis=0)
    two = lax.ppermute(one, "rows", swap)

    new_cols, gains, best = main_call(loc, one, two, aux, embeddings, factor_cols)
    peers = lax.all_to_all(best.reshape(NDEV, 1, 128), AXES, 0, 0)
    return new_cols, gains.reshape(rows_here), jnp.max(peers)


def solution(mesh):
    in_specs = (P(AXES, None), P(AXES, None), P(AXES), P())
    out_specs = (P(AXES, None), P(AXES), P())
    return jax.shard_map(body, mesh=mesh, in_specs=in_specs, out_specs=out_specs, check_vma=False)
```

```python
import functools

import jax
import jax.numpy as jnp
from jax import lax
from jax.experimental import pallas as pl
from jax.experimental.pallas import tpu as pltpu
from jax.sharding import PartitionSpec as P

PMAX = 16
EPS = 1e-06
TAU = 6.0
RIDGE = 1.0
AXES = ("rows", "cols")
NDEV = 128
CLASSES = 8
RING = 4
SUB = 4
NORM_TILES = 14
SOLVE_SUB = 4
GRANT = 58 << 20
LOG2E = 1.4426950408889634
TILES = 8
BS = 32
F32 = jnp.float32
BF16 = jnp.bfloat16


def iota(shape, dim):
    return lax.broadcasted_iota(jnp.int32, shape, dim)


def learn(c):
    return (c * (16.0 - c) + 8.0) / 72.0


def own_kernel(
    dev_ref, piv_s, piv_v, solved_ref, emb_ref, fac_ref, send_ref, loc_ref, ebuf, fbuf, sem
):
    rows_here, dim = emb_ref.shape
    k0 = fac_ref.shape[1]
    total = piv_s.shape[0]
    first = dev_ref[0] * rows_here
    pv = piv_v[...]
    before = jnp.sum((pv < first).astype(F32)).astype(jnp.int32)
    upto = jnp.sum((pv < first + rows_here).astype(F32)).astype(jnp.int32)
    mine = upto - before
    loc_ref[0] = before
    loc_ref[1] = mine
    idx = []
    copies = []
    for s in range(PMAX):
        p = piv_s[jnp.minimum(before + s, total - 1)]
        i = jnp.clip(p - first, 0, rows_here - 1)
        loc_ref[2 + s] = i
        idx.append(i)
        base = pl.multiple_of((i // 16) * 16, 16)
        c1 = pltpu.make_async_copy(
            emb_ref.at[pl.ds(base, 16), :], ebuf.at[pl.ds(16 * s, 16), :], sem.at[0, s]
        )
        c2 = pltpu.make_async_copy(
            fac_ref.at[pl.ds(base, 16), :], fbuf.at[pl.ds(16 * s, 16), :], sem.at[1, s]
        )
        c1.start()
        c2.start()
        copies += [c1, c2]
    r = iota((16, 16 * PMAX), 0)
    q = iota((16, 16 * PMAX), 1)
    rc = iota((16, 128), 0)
    lane = iota((16, 128), 1)
    hot = jnp.zeros((16, 16 * PMAX), F32)
    tag = jnp.zeros((16, 128), F32)
    for s in range(PMAX):
        j = before + s
        row = jnp.where(s < mine, 2 * lax.rem(j, CLASSES) + s // CLASSES, -1)
        hot = jnp.where((r == row) & (q == 16 * s + lax.rem(idx[s], 16)), 1.0, hot)
        line = solved_ref[pl.ds(idx[s] // 128, 1), :].astype(F32)
        here = iota((1, 128), 1) == lax.rem(idx[s], 128)
        c = jnp.sum(jnp.where(here, line, 0.0), axis=1, keepdims=True)
        tag = jnp.where(rc == row, jnp.where(lane == 0, c, (j + 1).astype(F32)), tag)
    hot = hot.astype(BF16)
    for c in copies:
        c.wait()
    e = jnp.dot(hot, ebuf[...], preferred_element_type=F32)
    f = jnp.dot(hot, fbuf[...], preferred_element_type=F32)
    row = jnp.concatenate([e, f, tag], axis=1)
    for k in range(CLASSES):
        send_ref[k, :, :] = row[2 * k : 2 * k + 2, :].astype(BF16)


def slots_kernel(cls_ref, *refs):
    out = refs[-1]
    slots, width = out.shape
    data = jnp.concatenate([ref[...] for ref in refs[:-1]], axis=0)
    ids = data[:, width - 127 : width - 126].astype(F32)
    want = (CLASSES * iota((data.shape[0], slots), 1) + cls_ref[0] + 1).astype(F32)
    hot = (ids == want).astype(BF16)
    out[...] = lax.dot_general(
        hot, data, (((0,), (0,)), ((), ())), preferred_element_type=F32
    ).astype(BF16)


def norms_kernel(first, solved_ref, emb_hbm, fac_hbm, *refs):
    aux_hbm, emb_ref, fac_ref, aux_ref, sem, out_sem = refs[-6:]
    rows, dim = emb_ref.shape
    tile = emb_hbm.shape[0] // NORM_TILES
    nchunk = tile // 128
    ey = iota((128, 128), 0) == iota((128, 128), 1)
    lane = iota((128, 128), 1)
    ndims = (((1,), (1,)), ((), ()))

    def fetch(t):
        src = pl.ds(pl.multiple_of((first + t) * tile, tile), tile)
        dst = pl.ds(pl.multiple_of(t * tile, tile), tile)
        return [
            pltpu.make_async_copy(x.at[src, :], y.at[dst, :], sem.at[k, t])
            for k, (x, y) in enumerate(((emb_hbm, emb_ref), (fac_hbm, fac_ref)))
        ]

    def store(t):
        src = pl.ds(pl.multiple_of(t * tile, tile), tile)
        dst = pl.ds(pl.multiple_of((first + t) * tile, tile), tile)
        return pltpu.make_async_copy(aux_ref.at[src, :], aux_hbm.at[dst, :], out_sem.at[t])

    for t in range(rows // tile):
        for c in fetch(t):
            c.start()

    def step(t, carry):
        st = solved_ref[pl.ds((first + t) * nchunk, nchunk), :].astype(F32)
        for c in fetch(t):
            c.wait()
        for c in range(nchunk):
            o = pl.ds(pl.multiple_of(t * tile + 128 * c, 128), 128)
            x = emb_ref[o, :].astype(F32)
            f = fac_ref[o, :]
            ff = lax.dot_general(f, f, ndims, preferred_element_type=F32)
            ss = jnp.sum(x * x, axis=1, keepdims=True)
            fs = jnp.sum(jnp.where(ey, ff, 0.0), axis=1, keepdims=True)
            a = 1.0 / jnp.sqrt(ss / dim + EPS)
            b = jnp.broadcast_to(st[c : c + 1, :], (128, 128))
            q = learn(jnp.sum(jnp.where(ey, b, 0.0), axis=1, keepdims=True))
            aux_ref[o, :] = jnp.where(
                lane == 0, q * q + RIDGE - fs, jnp.where(lane == 1, a, q)
            )
        store(t).start()
        return carry

    lax.fori_loop(0, rows // tile, step, 0)
    for t in range(rows // tile):
        store(t).wait()


def split3(x):
    h = x.astype(BF16)
    r = x - h.astype(F32)
    m = r.astype(BF16)
    l = (r - m.astype(F32)).astype(BF16)
    return h, m, l


def lanes(x, k):
    return jnp.broadcast_to(x[:, k : k + 1], x.shape)


def sublanes(x, k):
    return jnp.broadcast_to(x[k : k + 1, :], x.shape)


def eliminate(w, between):
    rows, width = w.shape
    groups = [
        [w[8 * g : 8 * g + 8, 128 * v : 128 * v + 128] for v in range(width // 128)]
        for g in range(rows // 8)
    ]
    srow = iota((8, 128), 0)
    done = []
    for t in range(rows // 8):
        cols = [lanes(groups[t][0], 8 * t + k) for k in range(8)]
        e = [[sublanes(cols[k], i) for k in range(i + 1)] for i in range(8)]
        below = {
            g: [lanes(groups[g][0], 8 * t + k) for k in range(8)]
            for g in range(t + 1, rows // 8)
        }
        tops = [[sublanes(x, j) for x in groups[t]] for j in range(8)]
        m = [[None] * 8 for _ in range(8)]
        n = [[None] * 8 for _ in range(8)]
        for k in range(8):
            inv = 1.0 / e[k][k]
            for i in range(k + 1, 8):
                m[i][k] = e[i][k] * inv
                for j in range(k + 1, i + 1):
                    e[i][j] = e[i][j] - m[i][k] * e[j][k]
            for j in range(k):
                acc = m[k][j]
                for l in range(j + 1, k):
                    acc = acc + m[k][l] * n[l][j]
                n[k][j] = -acc
        root = [1.0 / jnp.sqrt(e[k][k]) for k in range(8)]
        inv = [[root[i] * n[i][j] for j in range(i)] + [root[i]] for i in range(8)]
        cols = []
        for j in range(8):
            c = jnp.where(srow == j, inv[j][j], 0.0)
            for i in range(j + 1, 8):
                c = jnp.where(srow == i, inv[i][j], c)
            cols.append(c)
        out = []
        for v in range(width // 128):
            acc = cols[0] * tops[0][v]
            for j in range(1, 8):
                acc = acc + cols[j] * tops[j][v]
            out.append(acc)
        for g in range(t + 1, rows // 8):
            for j in range(8):
                c = below[g][0] * inv[j][0]
                for k in range(1, j + 1):
                    c = c + below[g][k] * inv[j][k]
                groups[g] = [x - c * sublanes(o, j) for x, o in zip(groups[g], out)]
        done.append(jnp.concatenate(out, axis=1))
        between(t)
    return jnp.concatenate(done, axis=0)


def main_kernel(
    loc_ref, one_ref, two_ref, aux_hbm, emb_hbm, fac_hbm,
    out_hbm, gains_ref, best_ref,
    piv, pvec, ar, minv, mt, panel, aux_ref, emb_ref, fac_ref, out_ref, raw_a, raw_b, sem, out_sem,
):
    rows_here, dim = emb_ref.shape
    tile = rows_here // TILES
    k0 = fac_ref.shape[1]
    n = piv.shape[0]

    def fetch(t):
        w = pl.ds(pl.multiple_of(t * tile, tile), tile)
        return [
            pltpu.make_async_copy(src.at[w, :], dst.at[w, :], sem.at[k, t])
            for k, (src, dst) in enumerate(
                ((aux_hbm, aux_ref), (emb_hbm, emb_ref), (fac_hbm, fac_ref))
            )
        ]

    for t in range(TILES):
        for c in fetch(t):
            c.start()

    nchunk = tile // 128
    sub = tile // SUB
    tdims = (((0,), (0,)), ((), ()))
    ndims = (((1,), (1,)), ((), ()))

    jj = iota((n, n), 0)
    qq = iota((n, n), 1)
    eye = (jj == qq).astype(F32)
    data = jnp.concatenate([one_ref[...], two_ref[...]], axis=0)
    ids = data[:, dim + k0 + 1 : dim + k0 + 2].astype(F32)
    permt = (ids == (qq + 1).astype(F32)).astype(BF16)
    v = lax.dot_general(permt, data, tdims, preferred_element_type=F32)
    pb = v.astype(BF16)
    piv[...] = pb[:, 0 : dim + k0]
    cs = 1.0 / jnp.sqrt(
        jnp.sum(v[:, 0:dim] * v[:, 0:dim], axis=1, keepdims=True) / dim + EPS
    )
    cq = learn(v[:, dim + k0 : dim + k0 + 1])
    rs = jnp.sum(eye * cs, axis=0, keepdims=True) * (TAU * LOG2E / dim)
    rq = jnp.sum(eye * cq, axis=0, keepdims=True)
    pvec[0:1, :] = rs
    pvec[1:2, :] = rq
    dots = lax.dot_general(pb[:, 0:dim], piv[:, 0:dim], ndims, preferred_element_type=F32)
    shared = lax.dot_general(
        pb[:, dim : dim + k0], piv[:, dim : dim + k0], ndims, preferred_element_type=F32
    )
    similar = jnp.exp2(dots * (cs * rs) - TAU * LOG2E)
    ar[:, 0:n] = similar * (cq * rq) + RIDGE * eye - shared
    ar[:, n : 2 * n] = eye

    def step(i, carry):
        for c in fetch(i):
            c.wait()
        def part_of_panel(c):
            w = pl.ds(pl.multiple_of(i * tile + sub * c, 16), sub)
            a = aux_ref[w, 1:2]
            q = aux_ref[w, 2:3]
            dots = lax.dot_general(
                emb_ref[w, :], piv[:, 0:dim], ndims, preferred_element_type=F32
            )
            shared = lax.dot_general(
                fac_ref[w, :], piv[:, dim : dim + k0], ndims, preferred_element_type=F32
            )
            similar = jnp.exp2(dots * (a * pvec[0:1, :]) - TAU * LOG2E)
            p = similar * (q * pvec[1:2, :]) - shared
            ph = p.astype(BF16)
            panel[w, 0:n] = ph
            panel[w, n : 2 * n] = (p - ph.astype(F32)).astype(BF16)

        rows = pl.ds(pl.multiple_of(i * BS, BS), BS)
        shift = lax.rem(n - i * BS, n)
        a = pltpu.roll(ar[rows, 0:n], shift, 1)
        w = eliminate(jnp.concatenate([a, ar[rows, n : 2 * n]], axis=1), part_of_panel)
        u = pltpu.roll(w[:, 0:n], i * BS, 1)
        m = w[:, n : 2 * n]
        minv[rows, :] = m
        uh, um, ul = split3(u)
        mh, mm, ml = split3(m)
        left = jnp.concatenate([uh, uh, um, uh, ul, um], axis=0)
        r_a = jnp.concatenate([uh, um, uh, ul, uh, um], axis=0)
        r_m = jnp.concatenate([mh, mm, mh, ml, mh, mm], axis=0)
        ar[:, 0:n] -= lax.dot_general(left, r_a, tdims, preferred_element_type=F32)
        ar[:, n : 2 * n] -= lax.dot_general(left, r_m, tdims, preferred_element_type=F32)
        return carry

    lax.fori_loop(0, TILES, step, 0)

    t = minv[...].T
    h = t.astype(BF16)
    mt[0:n, :] = h
    mt[n : 2 * n, :] = h
    mt[2 * n : 3 * n, :] = (t - h.astype(F32)).astype(BF16)
    best_ref[...] = jnp.full(best_ref.shape, -jnp.inf, F32)

    def ridge(s, carry):
        at = loc_ref[2 + s]
        w = pl.ds(pl.multiple_of((at // 16) * 16, 16), 16)
        p = panel[w, 0:n].astype(F32) + panel[w, n : 2 * n].astype(F32)
        here = (iota((16, n), 0) == lax.rem(at, 16)) & (iota((16, n), 1) == loc_ref[0] + s)
        p = p + jnp.where(here, RIDGE, 0.0)
        ph = p.astype(BF16)
        panel[w, 0:n] = ph
        panel[w, n : 2 * n] = (p - ph.astype(F32)).astype(BF16)
        return carry

    lax.fori_loop(0, jnp.minimum(loc_ref[1], PMAX), ridge, 0)

    def store(t):
        w = pl.ds(pl.multiple_of(t * tile, tile), tile)
        return pltpu.make_async_copy(out_ref.at[w, :], out_hbm.at[w, :], out_sem.at[t])

    part = tile // SOLVE_SUB
    ey = iota((128, 128), 0) == iota((128, 128), 1)

    def product(t, raw):
        for c in range(SOLVE_SUB):
            w = pl.ds(pl.multiple_of(t * tile + part * c, 16), part)
            both = jnp.concatenate([panel[w, :], panel[w, 0:n]], axis=1)
            raw[part * c : part * c + part, :] = jnp.dot(
                both, mt[...], preferred_element_type=F32
            )

    def finish(t, raw):
        lines = []
        for c in range(nchunk):
            full = raw[128 * c : 128 * c + 128, :]
            w = pl.ds(pl.multiple_of(t * tile + 128 * c, 128), 128)
            out_ref[w, :] = full.astype(BF16)
            g = aux_ref[w, 0:1] - jnp.sum(full * full, axis=1, keepdims=True)
            b = jnp.broadcast_to(g, (128, 128))
            lines.append(jnp.sum(jnp.where(ey, b, 0.0), axis=0, keepdims=True))
        lines = jnp.concatenate(lines, axis=0)
        gains_ref[pl.ds(t * nchunk, nchunk), :] = lines
        best_ref[...] = jnp.maximum(best_ref[...], jnp.max(lines, axis=0, keepdims=True))

    product(0, raw_a)

    def solve(t, carry):
        product(2 * t + 1, raw_b)
        finish(2 * t, raw_a)
        product(2 * t + 2, raw_a)
        finish(2 * t + 1, raw_b)
        store(2 * t).start()
        store(2 * t + 1).start()
        return carry

    lax.fori_loop(0, TILES // 2 - 1, solve, 0)
    product(TILES - 1, raw_b)
    finish(TILES - 2, raw_a)
    store(TILES - 2).start()
    finish(TILES - 1, raw_b)
    store(TILES - 1).start()
    for t in range(TILES):
        store(t).wait()


def main_call(loc, one, two, aux, embeddings, factor_cols):
    rows_here, dim = embeddings.shape
    k0 = factor_cols.shape[1]
    total = one.shape[0] + two.shape[0]
    tile = rows_here // TILES
    smem = pl.BlockSpec(memory_space=pltpu.SMEM)
    vmem = pl.BlockSpec(memory_space=pltpu.VMEM)
    hbm = pl.BlockSpec(memory_space=pltpu.HBM)
    return pl.pallas_call(
        main_kernel,
        out_shape=(
            jax.ShapeDtypeStruct((rows_here, total), BF16),
            jax.ShapeDtypeStruct((rows_here // 128, 128), F32),
            jax.ShapeDtypeStruct((NDEV, 128), F32),
        ),
        in_specs=[smem, vmem, vmem, hbm, hbm, hbm],
        out_specs=(hbm, vmem, vmem),
        scratch_shapes=[
            pltpu.VMEM((total, dim + k0), BF16),
            pltpu.VMEM((8, total), F32),
            pltpu.VMEM((total, 2 * total), F32),
            pltpu.VMEM((total, total), F32),
            pltpu.VMEM((3 * total, total), BF16),
            pltpu.VMEM((rows_here, 2 * total), BF16),
            pltpu.VMEM((rows_here, 128), F32),
            pltpu.VMEM((rows_here, dim), BF16),
            pltpu.VMEM((rows_here, k0), BF16),
            pltpu.VMEM((rows_here, total), BF16),
            pltpu.VMEM((tile, total), F32),
            pltpu.VMEM((tile, total), F32),
            pltpu.SemaphoreType.DMA((3, TILES)),
            pltpu.SemaphoreType.DMA((TILES,)),
        ],
        compiler_params=pltpu.CompilerParams(vmem_limit_bytes=50 << 20),
        name="panel_factor",
    )(loc, one, two, aux, embeddings, factor_cols)


def norms_part(solved2, embeddings, factor_cols, first, last, aux):
    rows_here, dim = embeddings.shape
    k0 = factor_cols.shape[1]
    tile = rows_here // NORM_TILES
    rows = (last - first) * tile
    hbm = pl.BlockSpec(memory_space=pltpu.HBM)
    specs = [pl.BlockSpec(memory_space=pltpu.VMEM), hbm, hbm]
    args = (solved2, embeddings, factor_cols)
    if aux is not None:
        specs.append(hbm)
        args += (aux,)
    return pl.pallas_call(
        functools.partial(norms_kernel, first),
        out_shape=jax.ShapeDtypeStruct((rows_here, 128), F32),
        in_specs=specs,
        out_specs=hbm,
        scratch_shapes=[
            pltpu.VMEM((rows, dim), BF16),
            pltpu.VMEM((rows, k0), BF16),
            pltpu.VMEM((rows, 128), F32),
            pltpu.SemaphoreType.DMA((2, last - first)),
            pltpu.SemaphoreType.DMA((last - first,)),
        ],
        input_output_aliases={} if aux is None else {3: 0},
        compiler_params=pltpu.CompilerParams(vmem_limit_bytes=GRANT),
        cost_estimate=pl.CostEstimate(
            flops=rows * (dim + k0) * 4, bytes_accessed=rows * (dim + k0) * 2, transcendentals=0
        ),
        name="row_norms",
    )(*args)


def ring(values, axis, pairs):
    return [lax.ppermute(v, axis, p) for v, p in zip(values, pairs)]


def body(embeddings, factor_cols, solved, pivots):
    rows_here, dim = embeddings.shape
    k0 = factor_cols.shape[1]
    total = pivots.shape[0]
    width = dim + k0 + 128
    tile = rows_here // TILES
    r = lax.axis_index("rows").astype(jnp.int32)
    c = lax.axis_index("cols").astype(jnp.int32)
    dev = (r * 16 + c).reshape(1)
    solved2 = solved.reshape(rows_here // 128, 128)
    piv2 = pivots.reshape(total // 128, 128)
    smem = pl.BlockSpec(memory_space=pltpu.SMEM)
    vmem = pl.BlockSpec(memory_space=pltpu.VMEM)
    hbm = pl.BlockSpec(memory_space=pltpu.HBM)
    small = pltpu.CompilerParams(vmem_limit_bytes=8 << 20)
    wide = lambda rows: jax.ShapeDtypeStruct((rows, width), BF16)
    swap = [(i, i ^ 1) for i in range(8)]
    zs = [[(i, i ^ (2 * k)) for i in range(8)] for k in range(1, RING)]
    xs = [[(i, i ^ (4 * k)) for i in range(16)] for k in range(1, RING)]
    ys = [[(i, i ^ k) for i in range(16)] for k in range(1, RING)]

    send, loc = pl.pallas_call(
        own_kernel,
        out_shape=(
            jax.ShapeDtypeStruct((CLASSES, 2, width), BF16),
            jax.ShapeDtypeStruct((2 + PMAX,), jnp.int32),
        ),
        in_specs=[smem, smem, vmem, vmem, hbm, hbm],
        out_specs=(vmem, smem),
        scratch_shapes=[
            pltpu.VMEM((16 * PMAX, dim), BF16),
            pltpu.VMEM((16 * PMAX, k0), BF16),
            pltpu.SemaphoreType.DMA((2, PMAX)),
        ],
        compiler_params=pltpu.CompilerParams(vmem_limit_bytes=GRANT),
        name="own_rows",
    )(dev, pivots, piv2, solved2, embeddings, factor_cols)
    mine = lax.all_to_all(send, "rows", 0, 0).reshape(16, width)
    counts, mine = lax.optimization_barrier((solved2, mine))
    got = [mine] + ring([mine] * 3, "cols", xs)
    aux = norms_part(counts, embeddings, factor_cols, 0, 5, None)
    aux, *got = lax.optimization_barrier((aux, *got))
    mine = pl.pallas_call(
        slots_kernel,
        out_shape=wide(total // CLASSES),
        in_specs=[smem] + [vmem] * RING,
        out_specs=vmem,
        compiler_params=small,
        name="slots",
    )(r.reshape(1), *got)
    counts, mine = lax.optimization_barrier((solved2, mine))
    got = [mine] + ring([mine] * 3, "cols", ys)
    aux = norms_part(counts, embeddings, factor_cols, 5, 10, aux)
    aux, *got = lax.optimization_barrier((aux, *got))
    mine = got[0] + got[1] + got[2] + got[3]
    counts, mine = lax.optimization_barrier((solved2, mine))
    got = [mine] + ring([mine] * 3, "rows", zs)
    aux = norms_part(counts, embeddings, factor_cols, 10, NORM_TILES, aux)
    aux, *got = lax.optimization_barrier((aux, *got))
    one = jnp.concatenate(got, axis=0)
    two = lax.ppermute(one, "rows", swap)

    new_cols, gains, best = main_call(loc, one, two, aux, embeddings, factor_cols)
    peers = lax.all_to_all(best.reshape(NDEV, 1, 128), AXES, 0, 0)
    return new_cols, gains.reshape(rows_here), jnp.max(peers)


def solution(mesh):
    in_specs = (P(AXES, None), P(AXES, None), P(AXES), P())
    out_specs = (P(AXES, None), P(AXES), P())
    return jax.shard_map(body, mesh=mesh, in_specs=in_specs, out_specs=out_specs, check_vma=False)
```
